256 devices in a mesh: slab: 8 (over y, core), grp: 32 (over x, z).
Axes of the slice: x: 4, y: 4, z: 8, core: 2. Of those that a mesh axis runs over, the one named last changes fastest.
Arguments:
- diag_jac: bfloat16 [3072, 625, 625], P(('slab', 'grp')), may hold values from -0.75 to 0.75
- xface_jac: bfloat16 [3072, 2, 15625], P(('slab', 'grp')), may hold values from -1.5 to 1.5
- side_jac: bfloat16 [3072, 4, 15625], P(('slab', 'grp')), may hold values from -1.5 to 1.5
- orient: int32 [3072], P(('slab', 'grp')), may hold values from 0 to 3
- owner: int32 [3072], P(('slab', 'grp')), may hold values from 0 to 7, as said below
Outputs:
- agglomerated: bfloat16 [16384, 7, 1600], P(('slab', 'grp'))
The draws below stay inside these ranges and needn't reach their ends.
Inputs may be any that keep to these rules, and one draw needn't show every extreme that they name: An element's owner is a grp index below 8 on its own slab. Among the 12 elements of one device at most 2 share an owner; on every slab one owner receives exactly 2 elements from every device of that slab.
All inputs are finite; a program needn't handle non-finite values.
Results may differ from the reference program's by a relative error of at most 0.001.
Values may be sent and summed in bfloat16 or wider, within the bound.
A program may use at most 64 MiB of HBM per device.

```python
import jax
import jax.numpy as jnp
import numpy as np
from jax import lax

NV = 5
PF = 4
PM = 2
PC = 1
E_DEV = 12
NF = 625
NFACE = 125
NCOARSE = 40
MOST = 2
SLOTS = 64
ELEMS = 3072
N_SLAB = 8
N_GRP = 32


def draw_owner(key, part):
    devices = N_SLAB * N_GRP
    owners_n = N_GRP // 4
    most = max(2, 3 * E_DEV // (2 * owners_n))
    full = jax.random.randint(jax.random.fold_in(key, 11), (N_SLAB,), 0, owners_n)
    full_dev = jnp.repeat(full, N_GRP)
    keys = jax.random.split(jax.random.fold_in(key, 12), devices)
    orders = jax.vmap(lambda single: jax.random.permutation(single, E_DEV))(keys)
    offsets = jax.random.randint(jax.random.fold_in(key, 13), (devices,), 0, owners_n - 1)
    places = jnp.arange(E_DEV, dtype=jnp.int32)[None, :]
    others = (full_dev[:, None] + 1 + (offsets[:, None] + places - most) % (owners_n - 1)) % owners_n
    values = jnp.where(places < most, full_dev[:, None], others)
    inverse = jnp.argsort(orders, axis=1)
    result = jnp.take_along_axis(values, inverse, axis=1)
    return result.reshape(-1).astype(jnp.int32)


def touch_ends(values, own_key, least, high):
    shape = values.shape
    index_at = [jax.random.randint(jax.random.fold_in(own_key, axis), (), 0, shape[axis]) for axis in range(len(shape))]
    values = values.at[tuple(index_at)].set(least)
    longest = shape.index(max(shape))
    index_at[longest] = (index_at[longest] + 1) % shape[longest]
    return values.at[tuple(index_at)].set(high)


def level_of(rng, shape, cuts, least, top_value):
    def one(position, shards_of):
        steps = jax.random.uniform(jax.random.fold_in(jax.random.fold_in(rng, 6), position), (shards_of,), jnp.float32, least / len(cuts), top_value / len(cuts))
        return jnp.repeat(jnp.exp(steps), shape[position] // shards_of).reshape((-1,) + (1,) * (len(shape) - position - 1))

    level = one(*cuts[0])
    for cut in cuts[1:]:
        level = level * one(*cut)
    return level


def scatter_about(rng, shape, deviation, reach, cuts=(), kind=jnp.bfloat16):
    values = jax.random.normal(rng, shape, jnp.float32) * deviation
    if len(cuts) > 0:
        values = level_of(rng, shape, cuts, -0.22, 0.18) * values
    return jnp.clip(values, min=-reach, max=reach).astype(kind)


def setup_inputs(seed: int = 0) -> dict:
    arg_keys = jax.random.split(jax.random.key(seed), 6)
    return {
        "diag_jac": scatter_about(arg_keys[0], (ELEMS, NF, NF), 0.125, 0.75, ((0, 256),)),
        "xface_jac": scatter_about(arg_keys[1], (ELEMS, 2, NFACE * NFACE), 0.25, 1.5, ((0, 256),)),
        "side_jac": scatter_about(arg_keys[2], (ELEMS, 4, NFACE * NFACE), 0.25, 1.5, ((0, 256),)),
        "orient": touch_ends(jax.random.randint(arg_keys[3], (ELEMS,), 0, 4), jax.random.fold_in(arg_keys[3], 1), 0, 3).astype(jnp.int32),
        "owner": draw_owner(jax.random.fold_in(arg_keys[5], 71), 0),
    }


def gll_points(degree):
    if degree == 1:
        return np.array([-1.0, 1.0])
    if degree == 2:
        return np.array([-1.0, 0.0, 1.0])
    if degree == 3:
        inner_pt = np.sqrt(0.2)
        return np.array([-1.0, -inner_pt, inner_pt, 1.0])
    inner_pt = np.sqrt(3.0 / 7.0)
    return np.array([-1.0, -inner_pt, 0.0, inner_pt, 1.0])

def lagrange(source_deg, target_deg):
    source = gll_points(source_deg)
    target = gll_points(target_deg)
    result = np.ones((target_deg + 1, source_deg + 1))
    for j in range(source_deg + 1):
        for m in range(source_deg + 1):
            if m != j:
                result[:, j] = result[:, j] * (target - source[m]) / (source[j] - source[m])
    return result

def grid_coords(nvars, side, dims):
    flat = np.arange(nvars * side ** dims)
    parts = []
    for power in range(dims, -1, -1):
        parts.append(flat // side ** power % (side if power < dims else nvars))
    return parts

def turn_table(nvars, side, with_x):
    if with_x:
        coords = grid_coords(nvars, side, 3)
        first, second = (coords[2], coords[3])
    else:
        coords = grid_coords(nvars, side, 2)
        first, second = (coords[1], coords[2])
    tables = []
    for turns in range(4):
        if with_x:
            index = ((coords[0] * side + coords[1]) * side + first) * side + second
        else:
            index = (coords[0] * side + first) * side + second
        tables.append(index)
        first, second = (side - 1 - second, first)
    return np.stack(tables).astype(np.int32)

def build_tables(nvars, fine_deg, mid_deg, coarse_deg):
    fine_mid = lagrange(mid_deg, fine_deg)
    mid_coarse = lagrange(coarse_deg, mid_deg)

    def cube(line):
        return np.kron(np.eye(nvars), np.kron(np.kron(line, line), line))
    upper = cube(fine_mid)
    lower = cube(mid_coarse)
    count = fine_deg + 1
    coords = grid_coords(nvars, count, 3)
    faces = []
    for axis_num in (1, 2, 3):
        for level in (0, fine_deg):
            faces.append(upper[coords[axis_num] == level])
    face_rows = np.stack(faces)
    coarse_turns = turn_table(nvars, coarse_deg + 1, True)
    face_turns = turn_table(nvars, count, False)
    return (upper.astype(np.float32), lower.astype(np.float32), face_rows.astype(np.float32), coarse_turns, face_turns)

def galerkin(blocks, left, right, lower):
    high = lax.Precision.HIGHEST
    inner = jnp.einsum('efab,fbm->efam', blocks.astype(jnp.float32), right, precision=high)
    middle = jnp.einsum('fan,efam->efnm', left, inner, precision=high)
    half = jnp.einsum('efnm,md->efnd', middle, lower, precision=high)
    return jnp.einsum('nc,efnd->efcd', lower, half, precision=high)

def reference(diag_jac, xface_jac, side_jac, orient, owner):
    upper, lower, face_rows, coarse_turns, face_turns = build_tables(NV, PF, PM, PC)
    upper = jnp.asarray(upper)
    lower = jnp.asarray(lower)
    face_rows = jnp.asarray(face_rows)
    coarse_turns = jnp.asarray(coarse_turns)
    devices = N_SLAB * N_GRP
    ncoarse = NCOARSE
    side_left = jnp.stack([face_rows[2], face_rows[3], face_rows[4], face_rows[5]])
    side_right = jnp.stack([face_rows[3], face_rows[2], face_rows[5], face_rows[4]])

    def per_device(items):
        diag, xface, side, turns = items
        xface = xface.reshape(E_DEV, 2, NFACE, NFACE)
        side = side.reshape(E_DEV, 4, NFACE, NFACE)
        perm = jnp.take(coarse_turns, turns, axis=0)
        diag_c = galerkin(diag[:, None], upper[None], upper[None], lower)[:, 0]
        plus_c = galerkin(xface[:, 0:1], face_rows[1:2], face_rows[0:1], lower)[:, 0]
        plus_c = jnp.take_along_axis(plus_c, perm[:, None, :], axis=2)
        sent = galerkin(xface[:, 1:2], face_rows[0:1], face_rows[1:2], lower)[:, 0]
        sent = jnp.take_along_axis(sent, perm[:, :, None], axis=1)
        side_c = galerkin(side, side_left, side_right, lower)
        return (diag_c, plus_c, sent, side_c)
    diag_c, plus_c, sent, side_c = lax.map(per_device, (diag_jac.reshape(devices, E_DEV, NF, NF), xface_jac.reshape(devices, E_DEV, 2, NFACE * NFACE), side_jac.reshape(devices, E_DEV, 4, NFACE * NFACE), orient.reshape(devices, E_DEV)))
    sent = sent.reshape(N_SLAB, N_GRP * E_DEV, ncoarse, ncoarse)
    minus_c = jnp.roll(sent, 1, axis=0).reshape(devices, E_DEV, ncoarse, ncoarse)
    rows = jnp.concatenate([diag_c[:, :, None], minus_c[:, :, None], plus_c[:, :, None], side_c], axis=2)
    rows = rows.astype(jnp.bfloat16).reshape(devices * E_DEV, 7, ncoarse * ncoarse)
    owners_dev = owner.reshape(devices, E_DEV)
    earlier = jnp.arange(E_DEV)[None, :] < jnp.arange(E_DEV)[:, None]
    same = owners_dev[:, :, None] == owners_dev[:, None, :]
    rank = lax.optimization_barrier(jnp.sum((same & earlier[None]).astype(jnp.int32), axis=2))
    device_ids = jnp.arange(devices, dtype=jnp.int32)
    slab_ids = (device_ids // N_GRP)[:, None]
    grp_ids = (device_ids % N_GRP)[:, None]
    flat = ((slab_ids * N_GRP + owners_dev) * SLOTS + grp_ids * MOST + rank).astype(jnp.int32)
    result = jnp.zeros((N_SLAB * N_GRP * SLOTS, 7, ncoarse * ncoarse), jnp.bfloat16)
    return result.at[flat.reshape(-1)].set(rows)
```

```python
import functools
import jax
import jax.numpy as jnp
import numpy as np
from jax import lax
from jax.experimental import pallas as pl
from jax.experimental.pallas import tpu as pltpu
from jax.sharding import PartitionSpec as P

NV = 5
MESH = pl.DeviceIdType.MESH
ANY = pl.ANY
F32 = jnp.float32
BF16 = jnp.bfloat16
LANE = 128
ELEMS = 12
NF = 625
FLAT = 15625
ROWS = 80
ZT = 20
FACE = NV * LANE
DIAG = 13 * LANE
TURNS = ([0, 1, 2, 3], [2, 0, 3, 1], [3, 2, 1, 0], [1, 3, 0, 2])


def gll_points(degree):
    if degree == 1:
        return np.array([-1.0, 1.0])
    if degree == 2:
        return np.array([-1.0, 0.0, 1.0])
    inner_pt = np.sqrt(3.0 / 7.0)
    return np.array([-1.0, -inner_pt, 0.0, inner_pt, 1.0])


def lagrange(source_deg, target_deg):
    source = gll_points(source_deg)
    target = gll_points(target_deg)
    result = np.ones((target_deg + 1, source_deg + 1))
    for j in range(source_deg + 1):
        for m in range(source_deg + 1):
            if m != j:
                result[:, j] = result[:, j] * (target - source[m]) / (source[j] - source[m])
    return result


def split(table):
    lead = table.astype(BF16).astype(np.float64)
    return lead, (table - lead).astype(BF16).astype(np.float64)


def tables():
    line = lagrange(2, 4) @ lagrange(1, 2)
    face = np.kron(line, line)
    wide = np.kron(np.eye(32), face)
    wb = np.zeros((992, 256))
    for part, table in enumerate(split(wide)):
        wb[96:896, part * LANE:(part + 1) * LANE] = table
    w2 = np.zeros((NV, 640, 256))
    for v in range(NV):
        off = (500 * v) % LANE
        for part, table in enumerate(split(np.kron(face, np.eye(20)))):
            w2[v, off:off + 500, part * LANE:part * LANE + 80] = table
    turn = np.zeros((LANE, 6 * LANE))
    for o in (1, 2, 3):
        for jj in range(4):
            for v in range(NV):
                for kk in range(4):
                    lane = jj * 20 + v * 4 + kk
                    turn[jj * 20 + v * 4 + TURNS[o][kk], (o - 1) * LANE + lane] = 1
                    turn[TURNS[o][jj] * 20 + v * 4 + kk, (o + 2) * LANE + lane] = 1
    cube = np.kron(np.eye(NV), np.kron(np.kron(line, line), line))
    right = np.zeros((3, NF, 256))
    lead, rest = split(cube)
    for m in range(3):
        right[m, :, 40 * m:40 * m + 40] = lead
        right[m, :, LANE + 40 * m:LANE + 40 * m + 40] = rest
    left = np.concatenate([lead.T, rest.T], axis=0)
    return [jnp.asarray(t.astype(BF16)) for t in (wb, w2, turn, right, left)]


def dot(a, b):
    return jnp.dot(a, b, preferred_element_type=F32)


def halves(value):
    lead = value.astype(BF16)
    return lead, (value - lead.astype(F32)).astype(BF16)


def iota(shape, dim):
    return lax.broadcasted_iota(jnp.int32, shape, dim)


def face_rows(x_ref, s_ref, wb_ref, w2_ref, xs, zz):
    xs[0:24, 0:FLAT] = x_ref[...].reshape(24, FLAT)
    xs[32:80, 0:FLAT] = s_ref[...].reshape(48, FLAT)
    xs[24:32, :] = jnp.zeros((8, xs.shape[1]), BF16)
    xs[:, FLAT:] = jnp.zeros((ROWS, xs.shape[1] - FLAT), BF16)
    for q in range(4):
        tiles = range(q, ZT, 4)
        starts = [(800 * j) // LANE * LANE for j in tiles]
        rows = jnp.concatenate([xs[:, s:s + 896] for s in starts], axis=0)
        prod = dot(rows, wb_ref[96 - 32 * q:992 - 32 * q, :])
        both = prod[:, :LANE] + prod[:, LANE:]
        for i, j in enumerate(tiles):
            lead, rest = halves(both[ROWS * i:ROWS * (i + 1)])
            zz[0:ROWS, LANE * j:LANE * (j + 1)] = lead
            zz[ROWS:2 * ROWS, LANE * j:LANE * (j + 1)] = rest
    out = []
    for v in range(NV):
        start = (500 * v) // LANE * LANE
        prod = dot(zz[:, start:start + 640], w2_ref[v])
        out.append(prod[:ROWS, :LANE] + prod[:ROWS, LANE:] + prod[ROWS:, :LANE])
    return out


def turned(out, turn_ref, orient_ref):
    x = jnp.concatenate([t[0:32].astype(BF16) for t in out], axis=0)
    prod = dot(x, turn_ref[...])
    row = lax.rem(iota((NV * 32, LANE), 0), 32)
    o = jnp.zeros((NV * 32, LANE), jnp.int32)
    for e in range(ELEMS):
        o = jnp.where(row // 2 == e, orient_ref[e], o)
    odd = lax.rem(row, 2)
    result = x.astype(F32)
    for k in (1, 2, 3):
        result = jnp.where((o == k) & (odd == 0), prod[:, (k - 1) * LANE:k * LANE], result)
        result = jnp.where((o == k) & (odd == 1), prod[:, (k + 2) * LANE:(k + 3) * LANE], result)
    result = result.astype(BF16)
    return jnp.concatenate([result[32 * v:32 * v + 32] for v in range(NV)], axis=1)


def placement(owner_ref):
    lane = iota((16, LANE), 1)
    sub = iota((16, LANE), 0)
    on_lane = jnp.full((16, LANE), -1, jnp.int32)
    on_sub = jnp.full((16, LANE), -2, jnp.int32)
    for e in range(ELEMS):
        on_lane = jnp.where(lane == e, owner_ref[e], on_lane)
        on_sub = jnp.where(sub == e, owner_ref[e], on_sub)
    same = jnp.where((on_lane == on_sub) & (sub < lane), 1, 0)
    rank = jnp.sum(same, axis=0, keepdims=True)
    dest = jnp.where(lane < ELEMS, 2 * on_lane + rank, -1)
    return jnp.where(dest == sub, 1.0, 0.0).astype(F32)


def diag_triple(t, dv, right_ref, left_ref, hs, gs):
    for r in range(0, NF, 320):
        n = min(320, NF - r)
        prod = dot(dv[3 * t, r:r + n, :], right_ref[0])
        for m in (1, 2):
            prod += dot(dv[3 * t + m, r:r + n, :], right_ref[m])
        hs[r:r + n, :LANE], hs[r:r + n, LANE:] = halves(prod[:, :LANE] + prod[:, LANE:])
    prod = dot(left_ref[...], hs[...])
    g = prod[0:40, :LANE] + prod[0:40, LANE:] + prod[40:80, :LANE]
    for m in range(3):
        e = 3 * t + m
        gs[40 * e:40 * e + 40, :] = g if m == 0 else pltpu.roll(g, LANE - 40 * m, 1)


def diag_rows(gs):
    lane = iota((ELEMS, LANE), 1)
    tiles = [jnp.zeros((ELEMS, LANE), F32) for _ in range(13)]
    for c in range(40):
        row = gs[pl.ds(c, ELEMS, stride=40), :]
        at, shift = divmod(40 * c, LANE)
        if shift:
            row = pltpu.roll(row, shift, 1)
        tiles[at] = jnp.where((lane >= shift) & (lane < shift + 40), row, tiles[at])
        if shift + 40 > LANE:
            tiles[at + 1] = jnp.where(lane < shift + 40 - LANE, row, tiles[at + 1])
    return jnp.concatenate(tiles, axis=1)
GRP = 32
OWNERS = 8
SLOTS = 64
FIRST = 5 * FACE
LAST = FACE + DIAG


def project_and_send(orient_ref, owner_ref, x_hbm, s_hbm, d_hbm, wb_hbm, w2_hbm, tu_hbm, ri_hbm, le_hbm,
                     first_out, last_out,
                     xv, sv, dv, wb, w2, tu, ri, le, xs, zz, hs, gs, sent, minus, first, last,
                     sem, own_sem, step_send, step_recv, first_send, first_recv, last_send, last_recv):
    slab, grp = lax.axis_index("slab"), lax.axis_index("grp")
    slabs = lax.axis_size("slab")
    after, before = lax.rem(slab + 1, slabs), lax.rem(slab + slabs - 1, slabs)
    is_owner = grp < OWNERS

    pairs = [(x_hbm, xv), (s_hbm, sv), (wb_hbm, wb), (w2_hbm, w2), (tu_hbm, tu), (ri_hbm, ri), (le_hbm, le)]
    copies = [pltpu.make_async_copy(a, b, sem.at[i]) for i, (a, b) in enumerate(pairs)]
    copies += [pltpu.make_async_copy(d_hbm.at[e], dv.at[e], sem.at[7 + e]) for e in range(ELEMS)]
    for c in copies:
        c.start()

    barrier = pltpu.get_barrier_semaphore()
    pl.semaphore_signal(barrier, inc=1, device_id=(before, grp), device_id_type=MESH)

    @pl.when(is_owner)
    def _():
        def greet(i, carry):
            @pl.when(i != grp)
            def _():
                pl.semaphore_signal(barrier, inc=1, device_id=(slab, i), device_id_type=MESH)
            return carry
        lax.fori_loop(0, GRP, greet, 0)

    def to_owner(src, dst, send, recv, o):
        return pltpu.make_async_remote_copy(
            src_ref=src.at[o], dst_ref=dst.at[grp], send_sem=send.at[o], recv_sem=recv.at[grp],
            device_id=(slab, o), device_id_type=MESH)

    def keep(src, dst, i):
        return pltpu.make_async_copy(src.at[lax.rem(grp, OWNERS)], dst.at[grp], own_sem.at[i])

    def scatter(src, dst, send, recv, i):
        for k in range(OWNERS):
            o = lax.rem(grp + k, OWNERS)

            @pl.when(o != grp)
            def _():
                to_owner(src, dst, send, recv, o).start()

            @pl.when(o == grp)
            def _():
                keep(src, dst, i).start()

    def settle(src, dst, send, recv, i):
        for k in range(OWNERS):
            o = lax.rem(grp + k, OWNERS)

            @pl.when(o != grp)
            def _():
                to_owner(src, dst, send, recv, o).wait_send()

            @pl.when(o == grp)
            def _():
                keep(src, dst, i).wait()

        @pl.when(is_owner)
        def _():
            def arrive(i, carry):
                @pl.when(i != grp)
                def _():
                    pltpu.make_async_remote_copy(
                        src_ref=src.at[0], dst_ref=dst.at[i], send_sem=send.at[0], recv_sem=recv.at[i],
                        device_id=(slab, grp), device_id_type=MESH).wait_recv()
                return carry
            lax.fori_loop(0, GRP, arrive, 0)

    place = placement(owner_ref)
    pb = place.astype(BF16)
    for c in copies[:4]:
        c.wait()
    out = face_rows(xv, sv, wb, w2, xs, zz)
    copies[4].wait()
    x_rows = turned(out, tu, orient_ref)
    pick = jnp.where((iota((16, 32), 1) == 2 * iota((16, 32), 0) + 1) & (iota((16, 32), 0) < ELEMS), 1.0, 0.0)
    sent[...] = dot(pick.astype(BF16), x_rows).astype(BF16)

    @pl.when(is_owner)
    def _():
        pl.semaphore_wait(barrier, OWNERS)

    @pl.when(jnp.logical_not(is_owner))
    def _():
        pl.semaphore_wait(barrier, OWNERS + 1)

    step = pltpu.make_async_remote_copy(
        src_ref=sent, dst_ref=minus, send_sem=step_send, recv_sem=step_recv,
        device_id=(after, grp), device_id_type=MESH)
    step.start()

    side_rows = jnp.concatenate([t[32:80].astype(BF16) for t in out], axis=1)
    all_rows = jnp.concatenate([x_rows, side_rows], axis=0)
    rr, ee = iota((LANE, ROWS), 1), iota((LANE, ROWS), 0)
    picks = [jnp.where((rr == 2 * ee) & (ee < ELEMS), 1.0, 0.0)]
    picks += [jnp.where((rr == 32 + 4 * ee + f) & (ee < ELEMS), 1.0, 0.0) for f in range(4)]
    who = jnp.concatenate([dot(pb, p.astype(BF16)) for p in picks], axis=0).astype(BF16)
    placed = dot(who, all_rows).astype(BF16)
    for k in range(5):
        first[:, :, FACE * k:FACE * (k + 1)] = placed[16 * k:16 * k + 16].reshape(OWNERS, 2, FACE)
    scatter(first, first_out, first_send, first_recv, 0)

    copies[5].wait()
    copies[6].wait()
    for t in range(4):
        for m in range(3):
            copies[7 + 3 * t + m].wait()
        diag_triple(t, dv, ri, le, hs, gs)
    step.wait()
    last[:, :, :FACE] = dot(pb[:, :16], minus[...]).astype(BF16).reshape(OWNERS, 2, FACE)
    rows = diag_rows(gs).astype(BF16)
    last[:, :, FACE:] = dot(pb[:, :ELEMS], rows).astype(BF16).reshape(OWNERS, 2, DIAG)
    scatter(last, last_out, last_send, last_recv, 1)
    settle(first, first_out, first_send, first_recv, 0)
    settle(last, last_out, last_send, last_recv, 1)


def expand_tables():
    sel = [[4 * h + a for a in range(4)] for h in (0, 1)]
    sel += [[4 * a + 2 * h + b for a in (0, 1) for b in (0, 1)] for h in (0, 1)]
    sel += [[4 * a + 2 * b + h for a in (0, 1) for b in (0, 1)] for h in (0, 1)]
    ends = ((0, 1), (1, 0), (2, 3), (3, 2), (4, 5), (5, 4))
    idx = np.full((8, 8, LANE), -1, np.int32)
    for k, (a, b) in enumerate(ends):
        for u in range(5):
            for n in range(LANE):
                c, d = divmod((LANE * u + n) % 320, 40)
                if c in sel[a] and d % 8 in sel[b]:
                    idx[k, u, n] = sel[a].index(c) * 20 + d // 8 * 4 + sel[b].index(d % 8)
    return jnp.asarray(idx.reshape(64, LANE))


def expand(first_ref, last_ref, idx_ref, out_hbm, ov, sem):
    slots = SLOTS
    owner = lax.axis_index("grp") < OWNERS
    copies = [pltpu.make_async_copy(ov.at[k], out_hbm.at[k], sem.at[k]) for k in range(7)]

    @pl.when(jnp.logical_not(owner))
    def _():
        for k in range(7):
            ov[k] = jnp.zeros((slots, 1600), BF16)
            copies[k].start()

    @pl.when(owner)
    def _():
        lane = iota((slots, LANE), 1)
        ov[0] = last_ref[:, :, FACE:].reshape(slots, DIAG)[:, :1600]
        copies[0].start()
        for k in range(6):
            src = last_ref[:, :, :FACE] if k == 0 else first_ref[:, :, FACE * (k - 1):FACE * k]
            vals = src.reshape(slots, FACE).astype(F32)
            tiles = [vals[:, LANE * v:LANE * (v + 1)] for v in range(NV)]
            for u in range(5):
                idx = jnp.broadcast_to(idx_ref[8 * k + u:8 * k + u + 1, :], (slots, LANE))
                take = jnp.maximum(idx, 0)
                for p in range(3):
                    if p == 2 and u > 2:
                        continue
                    got = [jnp.take_along_axis(tiles[v], take, axis=1, mode="promise_in_bounds")
                           for v in ([2 * p] if u < 2 or p == 2 else [2 * p + 1] if u > 2 else [2 * p, 2 * p + 1])]
                    val = got[0] if len(got) == 1 else jnp.where(lane < 64, got[0], got[1])
                    val = jnp.where(idx >= 0, val, 0.0).astype(BF16)
                    at = 640 * p + LANE * u
                    width = 64 if p == 2 and u == 2 else LANE
                    ov[k + 1, :, at:at + width] = val[:, :width]
            copies[k + 1].start()

    for c in copies:
        c.wait()


def call_k3(first, last):
    vm = pl.BlockSpec(memory_space=pltpu.VMEM)
    return pl.pallas_call(
        expand,
        out_shape=jax.ShapeDtypeStruct((7, 64, 1600), BF16),
        in_specs=[vm] * 3,
        out_specs=pl.BlockSpec(memory_space=ANY),
        scratch_shapes=[pltpu.VMEM((7, 64, 1600), BF16), pltpu.SemaphoreType.DMA((7,))],
        name="expand",
    )(first, last, expand_tables())


def shards(diag_jac, xface_jac, side_jac, orient, owner):
    tabs = tables()
    smem = pl.BlockSpec(memory_space=pltpu.SMEM)
    anys = pl.BlockSpec(memory_space=ANY)
    sds = jax.ShapeDtypeStruct
    dma = pltpu.SemaphoreType.DMA
    first, last = pl.pallas_call(
        project_and_send,
        out_shape=(sds((GRP, 2, FIRST), BF16), sds((GRP, 2, LAST), BF16)),
        in_specs=[smem, smem] + [anys] * 8,
        out_specs=(anys, anys),
        scratch_shapes=[pltpu.VMEM((ELEMS, 2, FLAT), BF16), pltpu.VMEM((ELEMS, 4, FLAT), BF16),
                        pltpu.VMEM((ELEMS, NF, NF), BF16)]
        + [pltpu.VMEM(t.shape, BF16) for t in tabs]
        + [pltpu.VMEM((ROWS, 16000), BF16), pltpu.VMEM((2 * ROWS, ZT * LANE), BF16),
           pltpu.VMEM((NF, 2 * LANE), BF16), pltpu.VMEM((480, LANE), F32),
           pltpu.VMEM((16, FACE), BF16), pltpu.VMEM((16, FACE), BF16),
           pltpu.VMEM((OWNERS, 2, FIRST), BF16), pltpu.VMEM((OWNERS, 2, LAST), BF16),
           dma((19,)), dma((2,)), dma, dma, dma((OWNERS,)), dma((GRP,)), dma((OWNERS,)), dma((GRP,))],
        compiler_params=pltpu.CompilerParams(collective_id=0, has_side_effects=True),
        name="project_and_send",
    )(orient, owner, xface_jac, side_jac, diag_jac, *tabs)
    planes = call_k3(first, last)
    return jnp.transpose(planes, (1, 0, 2))


def solution(mesh):
    split_all = P(("slab", "grp"), None, None)
    vector = P(("slab", "grp"))
    return jax.shard_map(shards, mesh=mesh, in_specs=(split_all, split_all, split_all, vector, vector),
                         out_specs=split_all, check_vma=False)
```

```python
import functools
import jax
import jax.numpy as jnp
import numpy as np
from jax import lax
from jax.experimental import pallas as pl
from jax.experimental.pallas import tpu as pltpu
from jax.sharding import PartitionSpec as P

NV = 5
MESH = pl.DeviceIdType.MESH
ANY = pl.ANY
F32 = jnp.float32
BF16 = jnp.bfloat16
LANE = 128
ELEMS = 12
NF = 625
FLAT = 15625
ROWS = 80
ZT = 20
TILED = NV * LANE
FACE = 400
DIAG = 13 * LANE
TURNS = ([0, 1, 2, 3], [2, 0, 3, 1], [3, 2, 1, 0], [1, 3, 0, 2])


def gll_points(degree):
    if degree == 1:
        return np.array([-1.0, 1.0])
    if degree == 2:
        return np.array([-1.0, 0.0, 1.0])
    inner_pt = np.sqrt(3.0 / 7.0)
    return np.array([-1.0, -inner_pt, 0.0, inner_pt, 1.0])


def lagrange(source_deg, target_deg):
    source = gll_points(source_deg)
    target = gll_points(target_deg)
    result = np.ones((target_deg + 1, source_deg + 1))
    for j in range(source_deg + 1):
        for m in range(source_deg + 1):
            if m != j:
                result[:, j] = result[:, j] * (target - source[m]) / (source[j] - source[m])
    return result


def split(table):
    lead = table.astype(BF16).astype(np.float64)
    return lead, (table - lead).astype(BF16).astype(np.float64)


def tables():
    line = lagrange(2, 4) @ lagrange(1, 2)
    face = np.kron(line, line)
    wide = np.kron(np.eye(32), face)
    wb = np.zeros((992, 256))
    for part, table in enumerate(split(wide)):
        wb[96:896, part * LANE:(part + 1) * LANE] = table
    w2 = np.zeros((512, 256))
    for part, table in enumerate(split(np.kron(face, np.eye(20)))):
        w2[:500, part * LANE:part * LANE + 80] = table
    turn = np.zeros((LANE, 6 * LANE))
    for o in (1, 2, 3):
        for jj in range(4):
            for v in range(NV):
                for kk in range(4):
                    lane = jj * 20 + v * 4 + kk
                    turn[jj * 20 + v * 4 + TURNS[o][kk], (o - 1) * LANE + lane] = 1
                    turn[TURNS[o][jj] * 20 + v * 4 + kk, (o + 2) * LANE + lane] = 1
    cube = np.kron(np.eye(NV), np.kron(np.kron(line, line), line))
    lead, rest = split(cube)
    right = np.zeros((NF, LANE))
    right[:, :40] = lead
    right[:, 40:80] = rest
    left = np.concatenate([lead.T, rest.T], axis=0)
    return [jnp.asarray(t.astype(BF16)) for t in (wb, w2, turn, right, left)]


def dot(a, b):
    return jnp.dot(a, b, preferred_element_type=F32)


def halves(value):
    lead = value.astype(BF16)
    return lead, (value - lead.astype(F32)).astype(BF16)


def iota(shape, dim):
    return lax.broadcasted_iota(jnp.int32, shape, dim)


def face_rows(x_ref, s_ref, wb_ref, w2_copy, w2_ref, xs, zf, zz):
    xs[0:24, 0:FLAT] = x_ref[...].reshape(24, FLAT)
    xs[32:80, 0:FLAT] = s_ref[...].reshape(48, FLAT)
    xs[24:32, :] = jnp.zeros((8, xs.shape[1]), BF16)
    xs[:, FLAT:] = jnp.zeros((ROWS, xs.shape[1] - FLAT), BF16)
    for q in range(4):
        tiles = range(q, ZT, 4)
        starts = [(800 * j) // LANE * LANE for j in tiles]
        rows = jnp.concatenate([xs[:, s:s + 896] for s in starts], axis=0)
        prod = dot(rows, wb_ref[96 - 32 * q:992 - 32 * q, :])
        for i, j in enumerate(tiles):
            part = prod[ROWS * i:ROWS * (i + 1)]
            zf[:, LANE * j:LANE * (j + 1)] = part[:, :LANE] + part[:, LANE:]
    lane = iota((ROWS, LANE), 1)
    for v in range(NV):
        first, off = divmod(500 * v, LANE)
        parts = [zf[:, LANE * (first + i):LANE * (first + i + 1)] for i in range(5 if off else 4)]
        if off:
            parts = [pltpu.roll(p, LANE - off, 1) for p in parts]
            parts = [jnp.where(lane < LANE - off, parts[i], parts[i + 1]) for i in range(4)]
        for i in range(4):
            lead, rest = halves(parts[i])
            at = 2 * ROWS * v
            zz[at:at + ROWS, LANE * i:LANE * (i + 1)] = lead
            zz[at + ROWS:at + 2 * ROWS, LANE * i:LANE * (i + 1)] = rest
    w2_copy.wait()
    prod = dot(zz[...], w2_ref[...])
    out = []
    for v in range(NV):
        lead, rest = prod[2 * ROWS * v:2 * ROWS * v + ROWS], prod[2 * ROWS * v + ROWS:2 * ROWS * (v + 1)]
        out.append(lead[:, :LANE] + lead[:, LANE:] + rest[:, :LANE])
    return out


def packed(placed, kinds):
    lane = iota((16, LANE), 1)
    tiles = [None] * (-(-FACE * kinds // LANE))
    for k in range(kinds):
        for v in range(NV):
            value = placed[16 * k:16 * k + 16, LANE * v:LANE * (v + 1)]
            at, shift = divmod(FACE * k + 80 * v, LANE)
            if shift:
                value = pltpu.roll(value, shift, 1)
            tiles[at] = value if shift == 0 else jnp.where(lane >= shift, value, tiles[at])
            if shift + 80 > LANE:
                tiles[at + 1] = value
    return jnp.concatenate(tiles, axis=1)


def turned(out, turn_ref, orient_ref):
    x = jnp.concatenate([t[0:32].astype(BF16) for t in out], axis=0)
    prod = dot(x, turn_ref[...])
    row = lax.rem(iota((NV * 32, LANE), 0), 32)
    o = jnp.zeros((NV * 32, LANE), jnp.int32)
    for e in range(ELEMS):
        o = jnp.where(row // 2 == e, orient_ref[e], o)
    odd = lax.rem(row, 2)
    result = x.astype(F32)
    for k in (1, 2, 3):
        result = jnp.where((o == k) & (odd == 0), prod[:, (k - 1) * LANE:k * LANE], result)
        result = jnp.where((o == k) & (odd == 1), prod[:, (k + 2) * LANE:(k + 3) * LANE], result)
    result = result.astype(BF16)
    return jnp.concatenate([result[32 * v:32 * v + 32] for v in range(NV)], axis=1)


def placement(owner_ref):
    lane = iota((16, LANE), 1)
    sub = iota((16, LANE), 0)
    on_lane = jnp.full((16, LANE), -1, jnp.int32)
    on_sub = jnp.full((16, LANE), -2, jnp.int32)
    for e in range(ELEMS):
        on_lane = jnp.where(lane == e, owner_ref[e], on_lane)
        on_sub = jnp.where(sub == e, owner_ref[e], on_sub)
    same = jnp.where((on_lane == on_sub) & (sub < lane), 1, 0)
    rank = jnp.sum(same, axis=0, keepdims=True)
    dest = jnp.where(lane < ELEMS, 2 * on_lane + rank, -1)
    return jnp.where(dest == sub, 1.0, 0.0).astype(F32)


def diag_triple(t, dv, right_ref, left_ref, hs, gs):
    for r in range(0, NF, 320):
        n = min(320, NF - r)
        prod = dot(dv[3 * t, r:r + n, :], right_ref[0])
        for m in (1, 2):
            prod += dot(dv[3 * t + m, r:r + n, :], right_ref[m])
        hs[r:r + n, :LANE], hs[r:r + n, LANE:] = halves(prod[:, :LANE] + prod[:, LANE:])
    prod = dot(left_ref[...], hs[...])
    g = prod[0:40, :LANE] + prod[0:40, LANE:] + prod[40:80, :LANE]
    for m in range(3):
        e = 3 * t + m
        gs[40 * e:40 * e + 40, :] = g if m == 0 else pltpu.roll(g, LANE - 40 * m, 1)


def diag_tables(right_ref, wide):
    base = right_ref[...].astype(F32)
    lane = iota((NF, LANE), 1)
    lead = jnp.where(lane < 40, base, 0.0)
    rest = jnp.where(lane < 40, pltpu.roll(base, LANE - 40, 1), 0.0)
    for m in range(3):
        wide[m, :, :LANE] = (pltpu.roll(lead, 40 * m, 1) if m else lead).astype(BF16)
        wide[m, :, LANE:] = (pltpu.roll(rest, 40 * m, 1) if m else rest).astype(BF16)


def diag_rows(gs, first):
    lane = iota((6, LANE), 1)
    tiles = [jnp.zeros((6, LANE), F32) for _ in range(13)]
    for c in range(40):
        row = gs[pl.ds(40 * first + c, 6, stride=40), :]
        at, shift = divmod(40 * c, LANE)
        if shift:
            row = pltpu.roll(row, shift, 1)
        tiles[at] = jnp.where((lane >= shift) & (lane < shift + 40), row, tiles[at])
        if shift + 40 > LANE:
            tiles[at + 1] = jnp.where(lane < shift + 40 - LANE, row, tiles[at + 1])
    return jnp.concatenate(tiles, axis=1).astype(BF16)


GRP = 32
OWNERS = 8
SLOTS = 64
FIRST = 2048
MIDDLE = 512


def project_and_send(orient_hbm, owner_hbm, x_hbm, s_hbm, d_hbm, wb_hbm, w2_hbm, tu_hbm, ri_hbm, le_hbm,
                     first_out, middle_out, last_out,
                     orient_ref, owner_ref, xv, sv, dv, wb, w2, tu, ri, le, wide, xs, zf, zz, hs, gs, half, sent, minus,
                     first, middle, last, sem, own_sem, step_send, step_recv,
                     first_send, first_recv, middle_send, middle_recv, last_send, last_recv):
    slab, grp = lax.axis_index("slab"), lax.axis_index("grp")
    slabs = lax.axis_size("slab")
    after, before = lax.rem(slab + 1, slabs), lax.rem(slab + slabs - 1, slabs)
    is_owner = grp < OWNERS

    pairs = [(ri_hbm, ri), (x_hbm, xv), (s_hbm, sv), (wb_hbm, wb), (w2_hbm, w2), (tu_hbm, tu), (le_hbm, le)]
    scalars = [pltpu.make_async_copy(orient_hbm, orient_ref, sem.at[19]), pltpu.make_async_copy(owner_hbm, owner_ref, sem.at[20])]
    copies = [pltpu.make_async_copy(a, b, sem.at[i]) for i, (a, b) in enumerate(pairs)]
    blocks = [pltpu.make_async_copy(d_hbm.at[e], dv.at[e], sem.at[7 + e]) for e in range(ELEMS)]
    for c in scalars + copies:
        c.start()

    barrier = pltpu.get_barrier_semaphore()
    pl.semaphore_signal(barrier, inc=1, device_id=(before, grp), device_id_type=MESH)

    @pl.when(is_owner)
    def _():
        def greet(i, carry):
            @pl.when(i != grp)
            def _():
                pl.semaphore_signal(barrier, inc=1, device_id=(slab, i), device_id_type=MESH)
            return carry
        lax.fori_loop(0, GRP, greet, 0)

    def to_owner(src, dst, send, recv, o):
        return pltpu.make_async_remote_copy(
            src_ref=src.at[o], dst_ref=dst.at[grp], send_sem=send.at[o], recv_sem=recv.at[grp],
            device_id=(slab, o), device_id_type=MESH)

    def keep(src, dst, i):
        return pltpu.make_async_copy(src.at[lax.rem(grp, OWNERS)], dst.at[grp], own_sem.at[i])

    def scatter(src, dst, send, recv, i):
        for k in range(OWNERS):
            o = lax.rem(grp + k, OWNERS)

            @pl.when(o != grp)
            def _():
                to_owner(src, dst, send, recv, o).start()

            @pl.when(o == grp)
            def _():
                keep(src, dst, i).start()

    def settle(src, dst, send, recv, i):
        for k in range(OWNERS):
            o = lax.rem(grp + k, OWNERS)

            @pl.when(o != grp)
            def _():
                to_owner(src, dst, send, recv, o).wait_send()

            @pl.when(o == grp)
            def _():
                keep(src, dst, i).wait()

        @pl.when(is_owner)
        def _():
            def arrive(i, carry):
                @pl.when(i != grp)
                def _():
                    pltpu.make_async_remote_copy(
                        src_ref=src.at[0], dst_ref=dst.at[i], send_sem=send.at[0], recv_sem=recv.at[i],
                        device_id=(slab, grp), device_id_type=MESH).wait_recv()
                return carry
            lax.fori_loop(0, GRP, arrive, 0)

    for c in scalars:
        c.wait()
    place = placement(owner_ref)
    pb = place.astype(BF16)
    pb_late = pltpu.roll(place, LANE - 6, 1).astype(BF16)
    copies[0].wait()
    diag_tables(ri, wide)
    for c in copies[1:4]:
        c.wait()
    for c in blocks:
        c.start()
    out = face_rows(xv, sv, wb, copies[4], w2, xs, zf, zz)
    copies[5].wait()
    x_rows = turned(out, tu, orient_ref)
    pick = jnp.where((iota((16, 32), 1) == 2 * iota((16, 32), 0) + 1) & (iota((16, 32), 0) < ELEMS), 1.0, 0.0)
    sent[...] = dot(pick.astype(BF16), x_rows).astype(BF16)

    @pl.when(is_owner)
    def _():
        pl.semaphore_wait(barrier, OWNERS)

    @pl.when(jnp.logical_not(is_owner))
    def _():
        pl.semaphore_wait(barrier, OWNERS + 1)

    step = pltpu.make_async_remote_copy(
        src_ref=sent, dst_ref=minus, send_sem=step_send, recv_sem=step_recv,
        device_id=(after, grp), device_id_type=MESH)
    step.start()

    side_rows = jnp.concatenate([t[32:80].astype(BF16) for t in out], axis=1)
    all_rows = jnp.concatenate([x_rows, side_rows], axis=0)
    rr, ee = iota((LANE, ROWS), 1), iota((LANE, ROWS), 0)
    picks = [jnp.where((rr == 2 * ee) & (ee < ELEMS), 1.0, 0.0)]
    picks += [jnp.where((rr == 32 + 4 * ee + f) & (ee < ELEMS), 1.0, 0.0) for f in range(4)]
    who = jnp.concatenate([dot(pb, p.astype(BF16)) for p in picks], axis=0).astype(BF16)
    first[...] = packed(dot(who, all_rows), 5).astype(BF16).reshape(OWNERS, 2, FIRST)
    scatter(first, first_out, first_send, first_recv, 0)

    copies[6].wait()
    for t in range(4):
        for m in range(3):
            blocks[3 * t + m].wait()
        diag_triple(t, dv, wide, le, hs, gs)
        if t == 1:
            half[...] = dot(pb[:, :6], diag_rows(gs, 0))
        if t == 2:
            step.wait()
            placed = dot(pb[:, :16], minus[...])
            middle[...] = packed(placed, 1).astype(BF16).reshape(OWNERS, 2, MIDDLE)
            scatter(middle, middle_out, middle_send, middle_recv, 1)
    placed = half[...] + dot(pb_late[:, :6], diag_rows(gs, 6))
    last[...] = placed.astype(BF16).reshape(OWNERS, 2, DIAG)
    scatter(last, last_out, last_send, last_recv, 2)
    settle(first, first_out, first_send, first_recv, 0)
    settle(middle, middle_out, middle_send, middle_recv, 1)
    settle(last, last_out, last_send, last_recv, 2)


def expand_tables():
    sel = [[4 * h + a for a in range(4)] for h in (0, 1)]
    sel += [[4 * a + 2 * h + b for a in (0, 1) for b in (0, 1)] for h in (0, 1)]
    sel += [[4 * a + 2 * b + h for a in (0, 1) for b in (0, 1)] for h in (0, 1)]
    ends = ((0, 1), (1, 0), (2, 3), (3, 2), (4, 5), (5, 4))
    rows, plan = [], []
    for k, (a, b) in enumerate(ends):
        source = np.full(13 * LANE, -1)
        for n in range(1600):
            c, d = divmod(n, 40)
            if c % 8 in sel[a] and d % 8 in sel[b]:
                source[n] = (FACE * max(k - 1, 0) + c // 8 * 80 + sel[a].index(c % 8) * 20
                             + d // 8 * 4 + sel[b].index(d % 8))
        for u in range(13):
            part = source[LANE * u:LANE * (u + 1)]
            for tile in sorted(set(part[part >= 0] // LANE)):
                plan.append((k, u, int(tile), len(rows)))
                rows.append(np.where(part // LANE == tile, part % LANE, -1))
    rows += [np.full(LANE, -1)] * (-len(rows) % 8)
    return plan, jnp.asarray(np.stack(rows).astype(np.int32))


def expand(plan, first_ref, middle_ref, last_ref, idx_ref, out_hbm, ov, sem):
    owner = lax.axis_index("grp") < OWNERS
    copies = [pltpu.make_async_copy(ov.at[k], out_hbm.at[k], sem.at[k]) for k in range(7)]

    @pl.when(jnp.logical_not(owner))
    def _():
        for k in range(7):
            ov[k] = jnp.zeros((SLOTS, 1600), BF16)
            copies[k].start()

    @pl.when(owner)
    def _():
        ov[0] = last_ref[...].reshape(SLOTS, DIAG)[:, :1600]
        copies[0].start()
        sources = [middle_ref[...].reshape(SLOTS, MIDDLE), first_ref[...].reshape(SLOTS, FIRST)]
        for k in range(6):
            source = sources[min(k, 1)]
            for u in range(13):
                value = jnp.zeros((SLOTS, LANE), F32)
                for _, _, tile, row in [p for p in plan if p[:2] == (k, u)]:
                    idx = jnp.broadcast_to(idx_ref[row:row + 1, :], (SLOTS, LANE))
                    part = source[:, LANE * tile:LANE * (tile + 1)].astype(F32)
                    got = jnp.take_along_axis(part, jnp.maximum(idx, 0), axis=1, mode="promise_in_bounds")
                    value = jnp.where(idx >= 0, got, value)
                width = min(LANE, 1600 - LANE * u)
                ov[k + 1, :, LANE * u:LANE * u + width] = value.astype(BF16)[:, :width]
            copies[k + 1].start()

    for c in copies:
        c.wait()


def call_expand(first, middle, last):
    vm = pl.BlockSpec(memory_space=pltpu.VMEM)
    plan, idx = expand_tables()
    return pl.pallas_call(
        functools.partial(expand, plan),
        out_shape=jax.ShapeDtypeStruct((7, SLOTS, 1600), BF16),
        in_specs=[vm] * 4,
        out_specs=pl.BlockSpec(memory_space=ANY),
        scratch_shapes=[pltpu.VMEM((7, SLOTS, 1600), BF16), pltpu.SemaphoreType.DMA((7,))],
        compiler_params=pltpu.CompilerParams(vmem_limit_bytes=16 << 20),
        name="expand",
    )(first, middle, last, idx)


def shards(diag_jac, xface_jac, side_jac, orient, owner):
    tabs = tables()
    anys = pl.BlockSpec(memory_space=ANY)
    sds = jax.ShapeDtypeStruct
    dma = pltpu.SemaphoreType.DMA
    pieces = pl.pallas_call(
        project_and_send,
        out_shape=(sds((GRP, 2, FIRST), BF16), sds((GRP, 2, MIDDLE), BF16), sds((GRP, 2, DIAG), BF16)),
        in_specs=[pl.BlockSpec(memory_space=pltpu.HBM)] * 10,
        out_specs=(anys, anys, anys),
        scratch_shapes=[pltpu.SMEM((ELEMS,), jnp.int32), pltpu.SMEM((ELEMS,), jnp.int32),
                        pltpu.VMEM((ELEMS, 2, FLAT), BF16), pltpu.VMEM((ELEMS, 4, FLAT), BF16),
                        pltpu.VMEM((ELEMS, NF, NF), BF16)]
        + [pltpu.VMEM(t.shape, BF16) for t in tabs]
        + [pltpu.VMEM((3, NF, 2 * LANE), BF16), pltpu.VMEM((ROWS, 16000), BF16), pltpu.VMEM((ROWS, ZT * LANE), F32),
           pltpu.VMEM((NV * 2 * ROWS, 512), BF16), pltpu.VMEM((NF, 2 * LANE), BF16), pltpu.VMEM((480, LANE), F32),
           pltpu.VMEM((16, DIAG), F32), pltpu.VMEM((16, TILED), BF16), pltpu.VMEM((16, TILED), BF16),
           pltpu.VMEM((OWNERS, 2, FIRST), BF16), pltpu.VMEM((OWNERS, 2, MIDDLE), BF16), pltpu.VMEM((OWNERS, 2, DIAG), BF16),
           dma((21,)), dma((3,)), dma, dma, dma((OWNERS,)), dma((GRP,)), dma((OWNERS,)), dma((GRP,)),
           dma((OWNERS,)), dma((GRP,))],
        compiler_params=pltpu.CompilerParams(collective_id=0, has_side_effects=True, vmem_limit_bytes=40 << 20),
        name="project_and_send",
    )(*[pltpu.with_memory_space_constraint(a, pltpu.HBM)
        for a in (orient, owner, xface_jac, side_jac, diag_jac, *tabs)])
    planes = call_expand(*pieces)
    return jnp.transpose(planes, (1, 0, 2))


def solution(mesh):
    split_all = P(("slab", "grp"), None, None)
    vector = P(("slab", "grp"))
    return jax.shard_map(shards, mesh=mesh, in_specs=(split_all, split_all, split_all, vector, vector),
                         out_specs=split_all, check_vma=False)
```

```python
import functools
import jax
import jax.numpy as jnp
import numpy as np
from jax import lax
from jax.experimental import pallas as pl
from jax.experimental.pallas import tpu as pltpu
from jax.sharding import PartitionSpec as P

NV = 5
MESH = pl.DeviceIdType.MESH
ANY = pl.ANY
F32 = jnp.float32
BF16 = jnp.bfloat16
LANE = 128
ELEMS = 12
NF = 625
FLAT = 15625
ROWS = 80
ZT = 20
TILED = NV * LANE
FACE = 400
DIAG = 13 * LANE
TURNS = ([0, 1, 2, 3], [2, 0, 3, 1], [3, 2, 1, 0], [1, 3, 0, 2])


def gll_points(degree):
    if degree == 1:
        return np.array([-1.0, 1.0])
    if degree == 2:
        return np.array([-1.0, 0.0, 1.0])
    inner_pt = np.sqrt(3.0 / 7.0)
    return np.array([-1.0, -inner_pt, 0.0, inner_pt, 1.0])


def lagrange(source_deg, target_deg):
    source = gll_points(source_deg)
    target = gll_points(target_deg)
    result = np.ones((target_deg + 1, source_deg + 1))
    for j in range(source_deg + 1):
        for m in range(source_deg + 1):
            if m != j:
                result[:, j] = result[:, j] * (target - source[m]) / (source[j] - source[m])
    return result


def split(table):
    lead = table.astype(BF16).astype(np.float64)
    return lead, (table - lead).astype(BF16).astype(np.float64)


def tables():
    line = lagrange(2, 4) @ lagrange(1, 2)
    face = np.kron(line, line)
    wide = np.kron(np.eye(32), face)
    wb = np.zeros((992, 256))
    for part, table in enumerate(split(wide)):
        wb[96:896, part * LANE:(part + 1) * LANE] = table
    w2 = np.zeros((512, 256))
    for part, table in enumerate(split(np.kron(face, np.eye(20)))):
        w2[:500, part * LANE:part * LANE + 80] = table
    turn = np.zeros((LANE, 6 * LANE))
    for o in (1, 2, 3):
        for jj in range(4):
            for v in range(NV):
                for kk in range(4):
                    lane = jj * 20 + v * 4 + kk
                    turn[jj * 20 + v * 4 + TURNS[o][kk], (o - 1) * LANE + lane] = 1
                    turn[TURNS[o][jj] * 20 + v * 4 + kk, (o + 2) * LANE + lane] = 1
    cube = np.kron(np.eye(NV), np.kron(np.kron(line, line), line))
    lead, rest = split(cube)
    right = np.zeros((NF, 2 * LANE))
    right[:, :40] = lead
    right[:, LANE:LANE + 40] = rest
    left = np.concatenate([lead.T, rest.T], axis=0)
    return [jnp.asarray(t.astype(BF16)) for t in (wb, w2, turn, right, left)]


def dot(a, b):
    return jnp.dot(a, b, preferred_element_type=F32)


def halves(value):
    lead = value.astype(BF16)
    return lead, (value - lead.astype(F32)).astype(BF16)


def iota(shape, dim):
    return lax.broadcasted_iota(jnp.int32, shape, dim)


def face_rows(x_ref, s_ref, wb_ref, w2_copy, w2_ref, xs, zf, zz):
    xs[0:24, 0:FLAT] = x_ref[...].reshape(24, FLAT)
    xs[32:80, 0:FLAT] = s_ref[...].reshape(48, FLAT)
    xs[24:32, :] = jnp.zeros((8, xs.shape[1]), BF16)
    xs[:, FLAT:] = jnp.zeros((ROWS, xs.shape[1] - FLAT), BF16)
    for q in range(4):
        tiles = range(q, ZT, 4)
        starts = [(800 * j) // LANE * LANE for j in tiles]
        rows = jnp.concatenate([xs[:, s:s + 896] for s in starts], axis=0)
        prod = dot(rows, wb_ref[96 - 32 * q:992 - 32 * q, :])
        for i, j in enumerate(tiles):
            part = prod[ROWS * i:ROWS * (i + 1)]
            zf[:, LANE * j:LANE * (j + 1)] = part[:, :LANE] + part[:, LANE:]
    lane = iota((ROWS, LANE), 1)
    for v in range(NV):
        first, off = divmod(500 * v, LANE)
        parts = [zf[:, LANE * (first + i):LANE * (first + i + 1)] for i in range(5 if off else 4)]
        if off:
            parts = [pltpu.roll(p, LANE - off, 1) for p in parts]
            parts = [jnp.where(lane < LANE - off, parts[i], parts[i + 1]) for i in range(4)]
        for i in range(4):
            lead, rest = halves(parts[i])
            at = 2 * ROWS * v
            zz[at:at + ROWS, LANE * i:LANE * (i + 1)] = lead
            zz[at + ROWS:at + 2 * ROWS, LANE * i:LANE * (i + 1)] = rest
    w2_copy.wait()
    prod = dot(zz[...], w2_ref[...])
    out = []
    for v in range(NV):
        lead, rest = prod[2 * ROWS * v:2 * ROWS * v + ROWS], prod[2 * ROWS * v + ROWS:2 * ROWS * (v + 1)]
        out.append(lead[:, :LANE] + lead[:, LANE:] + rest[:, :LANE])
    return out


def packed(placed, kinds):
    lane = iota((16, LANE), 1)
    tiles = [None] * (-(-FACE * kinds // LANE))
    for k in range(kinds):
        for v in range(NV):
            value = placed[16 * k:16 * k + 16, LANE * v:LANE * (v + 1)]
            at, shift = divmod(FACE * k + 80 * v, LANE)
            if shift:
                value = pltpu.roll(value, shift, 1)
            tiles[at] = value if shift == 0 else jnp.where(lane >= shift, value, tiles[at])
            if shift + 80 > LANE:
                tiles[at + 1] = value
    return jnp.concatenate(tiles, axis=1)


def turned(out, turn_ref, orient_ref):
    x = jnp.concatenate([t[0:32].astype(BF16) for t in out], axis=0)
    prod = dot(x, turn_ref[...])
    row = lax.rem(iota((NV * 32, LANE), 0), 32)
    o = jnp.zeros((NV * 32, LANE), jnp.int32)
    for e in range(ELEMS):
        o = jnp.where(row // 2 == e, orient_ref[e], o)
    odd = lax.rem(row, 2)
    result = x.astype(F32)
    for k in (1, 2, 3):
        result = jnp.where((o == k) & (odd == 0), prod[:, (k - 1) * LANE:k * LANE], result)
        result = jnp.where((o == k) & (odd == 1), prod[:, (k + 2) * LANE:(k + 3) * LANE], result)
    result = result.astype(BF16)
    return jnp.concatenate([result[32 * v:32 * v + 32] for v in range(NV)], axis=1)


def placement(owner_ref):
    lane = iota((16, LANE), 1)
    sub = iota((16, LANE), 0)
    on_lane = jnp.full((16, LANE), -1, jnp.int32)
    on_sub = jnp.full((16, LANE), -2, jnp.int32)
    for e in range(ELEMS):
        on_lane = jnp.where(lane == e, owner_ref[e], on_lane)
        on_sub = jnp.where(sub == e, owner_ref[e], on_sub)
    same = jnp.where((on_lane == on_sub) & (sub < lane), 1, 0)
    rank = jnp.sum(same, axis=0, keepdims=True)
    dest = jnp.where(lane < ELEMS, 2 * on_lane + rank, -1)
    return jnp.where(dest == sub, 1.0, 0.0).astype(F32)


def diag_left(e, dv, left_ref, hs, slot, i):
    prod = dot(left_ref[...], dv[e])
    lead, rest = halves(prod[0:40] + prod[40:80])
    hs[slot, 80 * i:80 * i + 40, :] = lead
    hs[slot, 80 * i + 40:80 * i + 80, :] = rest


def diag_right(first, count, hs, slot, right_ref, gs):
    prod = dot(hs[slot], right_ref[...])
    for i in range(count):
        lead, rest = prod[80 * i:80 * i + 40], prod[80 * i + 40:80 * i + 80]
        e = first + i
        gs[40 * e:40 * e + 40, :] = lead[:, :LANE] + lead[:, LANE:] + rest[:, :LANE]


def diag_rows(gs, first):
    lane = iota((6, LANE), 1)
    tiles = [jnp.zeros((6, LANE), F32) for _ in range(13)]
    for c in range(40):
        row = gs[pl.ds(40 * first + c, 6, stride=40), :]
        at, shift = divmod(40 * c, LANE)
        if shift:
            row = pltpu.roll(row, shift, 1)
        tiles[at] = jnp.where((lane >= shift) & (lane < shift + 40), row, tiles[at])
        if shift + 40 > LANE:
            tiles[at + 1] = jnp.where(lane < shift + 40 - LANE, row, tiles[at + 1])
    return jnp.concatenate(tiles, axis=1).astype(BF16)


GRP = 32
OWNERS = 8
SLOTS = 64
FIRST = 2048
MIDDLE = 512
GROUP = 3


def project_and_send(orient_hbm, owner_hbm, x_hbm, s_hbm, d_hbm, wb_hbm, w2_hbm, tu_hbm, ri_hbm, le_hbm,
                     first_out, middle_out, last_out,
                     orient_ref, owner_ref, xv, sv, dv, wb, w2, tu, ri, le, xs, zf, zz, hs, gs, half, sent, minus,
                     first, middle, last, sem, own_sem, step_send, step_recv,
                     first_send, first_recv, middle_send, middle_recv, last_send, last_recv):
    slab, grp = lax.axis_index("slab"), lax.axis_index("grp")
    slabs = lax.axis_size("slab")
    after, before = lax.rem(slab + 1, slabs), lax.rem(slab + slabs - 1, slabs)
    is_owner = grp < OWNERS

    pairs = [(x_hbm, xv), (s_hbm, sv), (wb_hbm, wb), (w2_hbm, w2), (tu_hbm, tu), (le_hbm, le), (ri_hbm, ri)]
    scalars = [pltpu.make_async_copy(orient_hbm, orient_ref, sem.at[19]), pltpu.make_async_copy(owner_hbm, owner_ref, sem.at[20])]
    copies = [pltpu.make_async_copy(a, b, sem.at[i]) for i, (a, b) in enumerate(pairs)]
    blocks = [pltpu.make_async_copy(d_hbm.at[e], dv.at[e], sem.at[7 + e]) for e in range(ELEMS)]
    for c in scalars + copies:
        c.start()

    barrier = pltpu.get_barrier_semaphore()
    pl.semaphore_signal(barrier, inc=1, device_id=(before, grp), device_id_type=MESH)

    @pl.when(is_owner)
    def _():
        def greet(i, carry):
            @pl.when(i != grp)
            def _():
                pl.semaphore_signal(barrier, inc=1, device_id=(slab, i), device_id_type=MESH)
            return carry
        lax.fori_loop(0, GRP, greet, 0)

    def to_owner(src, dst, send, recv, o):
        return pltpu.make_async_remote_copy(
            src_ref=src.at[o], dst_ref=dst.at[grp], send_sem=send.at[o], recv_sem=recv.at[grp],
            device_id=(slab, o), device_id_type=MESH)

    def keep(src, dst, i):
        return pltpu.make_async_copy(src.at[lax.rem(grp, OWNERS)], dst.at[grp], own_sem.at[i])

    def scatter(src, dst, send, recv, i):
        for k in range(1, OWNERS):
            to_owner(src, dst, send, recv, lax.rem(grp + k, OWNERS)).start()

        @pl.when(is_owner)
        def _():
            keep(src, dst, i).start()

        @pl.when(jnp.logical_not(is_owner))
        def _():
            to_owner(src, dst, send, recv, lax.rem(grp, OWNERS)).start()

    def settle(src, dst, send, recv, i):
        for k in range(1, OWNERS):
            to_owner(src, dst, send, recv, lax.rem(grp + k, OWNERS)).wait_send()

        @pl.when(is_owner)
        def _():
            keep(src, dst, i).wait()
            for k in range(1, GRP):
                pltpu.make_async_remote_copy(
                    src_ref=src.at[0], dst_ref=dst.at[lax.rem(grp + k, GRP)], send_sem=send.at[0],
                    recv_sem=recv.at[lax.rem(grp + k, GRP)], device_id=(slab, grp), device_id_type=MESH).wait_recv()

        @pl.when(jnp.logical_not(is_owner))
        def _():
            to_owner(src, dst, send, recv, lax.rem(grp, OWNERS)).wait_send()

    for c in scalars:
        c.wait()
    place = placement(owner_ref)
    pb = place.astype(BF16)
    pb_late = pltpu.roll(place, LANE - 6, 1).astype(BF16)
    for c in copies[:3]:
        c.wait()
    for c in blocks:
        c.start()
    out = face_rows(xv, sv, wb, copies[3], w2, xs, zf, zz)
    copies[4].wait()
    x_rows = turned(out, tu, orient_ref)
    pick = jnp.where((iota((16, 32), 1) == 2 * iota((16, 32), 0) + 1) & (iota((16, 32), 0) < ELEMS), 1.0, 0.0)
    sent[...] = dot(pick.astype(BF16), x_rows).astype(BF16)

    @pl.when(is_owner)
    def _():
        pl.semaphore_wait(barrier, OWNERS)

    @pl.when(jnp.logical_not(is_owner))
    def _():
        pl.semaphore_wait(barrier, OWNERS + 1)

    step = pltpu.make_async_remote_copy(
        src_ref=sent, dst_ref=minus, send_sem=step_send, recv_sem=step_recv,
        device_id=(after, grp), device_id_type=MESH)
    step.start()

    side_rows = jnp.concatenate([t[32:80].astype(BF16) for t in out], axis=1)
    all_rows = jnp.concatenate([x_rows, side_rows], axis=0)
    rr, ee = iota((LANE, ROWS), 1), iota((LANE, ROWS), 0)
    picks = [jnp.where((rr == 2 * ee) & (ee < ELEMS), 1.0, 0.0)]
    picks += [jnp.where((rr == 32 + 4 * ee + f) & (ee < ELEMS), 1.0, 0.0) for f in range(4)]
    who = jnp.concatenate([dot(pb, p.astype(BF16)) for p in picks], axis=0).astype(BF16)
    first[...] = packed(dot(who, all_rows), 5).astype(BF16).reshape(OWNERS, 2, FIRST)
    scatter(first, first_out, first_send, first_recv, 0)

    copies[5].wait()
    copies[6].wait()
    groups = ELEMS // GROUP
    for t in range(groups + 1):
        if t < groups:
            for i in range(GROUP):
                blocks[GROUP * t + i].wait()
            for i in range(GROUP):
                diag_left(GROUP * t + i, dv, le, hs, t % 2, i)
        if t > 0:
            diag_right(GROUP * (t - 1), GROUP, hs, (t - 1) % 2, ri, gs)
        if GROUP * t == 6:
            half[...] = dot(pb[:, :6], diag_rows(gs, 0))
        if t == groups - 1:
            step.wait()
            placed = dot(pb[:, :16], minus[...])
            middle[...] = packed(placed, 1).astype(BF16).reshape(OWNERS, 2, MIDDLE)
            scatter(middle, middle_out, middle_send, middle_recv, 1)
    placed = half[...] + dot(pb_late[:, :6], diag_rows(gs, 6))
    last[...] = placed.astype(BF16).reshape(OWNERS, 2, DIAG)
    scatter(last, last_out, last_send, last_recv, 2)
    settle(first, first_out, first_send, first_recv, 0)
    settle(middle, middle_out, middle_send, middle_recv, 1)
    settle(last, last_out, last_send, last_recv, 2)


def expand_tables():
    sel = [[4 * h + a for a in range(4)] for h in (0, 1)]
    sel += [[4 * a + 2 * h + b for a in (0, 1) for b in (0, 1)] for h in (0, 1)]
    sel += [[4 * a + 2 * b + h for a in (0, 1) for b in (0, 1)] for h in (0, 1)]
    ends = ((0, 1), (1, 0), (2, 3), (3, 2), (4, 5), (5, 4))
    rows, plan = [], []
    for k, (a, b) in enumerate(ends):
        source = np.full(13 * LANE, -1)
        for n in range(1600):
            c, d = divmod(n, 40)
            if c % 8 in sel[a] and d % 8 in sel[b]:
                source[n] = (FACE * max(k - 1, 0) + c // 8 * 80 + sel[a].index(c % 8) * 20
                             + d // 8 * 4 + sel[b].index(d % 8))
        for u in range(13):
            part = source[LANE * u:LANE * (u + 1)]
            for tile in sorted(set(part[part >= 0] // LANE)):
                plan.append((k, u, int(tile), len(rows)))
                rows.append(np.where(part // LANE == tile, part % LANE, -1))
    rows += [np.full(LANE, -1)] * (-len(rows) % 8)
    return plan, jnp.asarray(np.stack(rows).astype(np.int32))


def expand(plan, first_ref, middle_ref, last_ref, idx_ref, out_hbm, ov, sem):
    owner = lax.axis_index("grp") < OWNERS
    copies = [pltpu.make_async_copy(ov.at[k], out_hbm.at[k], sem.at[k]) for k in range(7)]

    @pl.when(jnp.logical_not(owner))
    def _():
        for k in range(7):
            ov[k] = jnp.zeros((SLOTS, 1600), BF16)
            copies[k].start()

    @pl.when(owner)
    def _():
        ov[0] = last_ref[...].reshape(SLOTS, DIAG)[:, :1600]
        copies[0].start()
        sources = [middle_ref[...].reshape(SLOTS, MIDDLE), first_ref[...].reshape(SLOTS, FIRST)]
        for k in range(6):
            source = sources[min(k, 1)]
            for u in range(13):
                value = jnp.zeros((SLOTS, LANE), F32)
                for _, _, tile, row in [p for p in plan if p[:2] == (k, u)]:
                    idx = jnp.broadcast_to(idx_ref[row:row + 1, :], (SLOTS, LANE))
                    part = source[:, LANE * tile:LANE * (tile + 1)].astype(F32)
                    got = jnp.take_along_axis(part, jnp.maximum(idx, 0), axis=1, mode="promise_in_bounds")
                    value = jnp.where(idx >= 0, got, value)
                width = min(LANE, 1600 - LANE * u)
                ov[k + 1, :, LANE * u:LANE * u + width] = value.astype(BF16)[:, :width]
            copies[k + 1].start()

    for c in copies:
        c.wait()


def call_expand(first, middle, last):
    vm = pl.BlockSpec(memory_space=pltpu.VMEM)
    plan, idx = expand_tables()
    return pl.pallas_call(
        functools.partial(expand, plan),
        out_shape=jax.ShapeDtypeStruct((7, SLOTS, 1600), BF16),
        in_specs=[vm] * 4,
        out_specs=pl.BlockSpec(memory_space=ANY),
        scratch_shapes=[pltpu.VMEM((7, SLOTS, 1600), BF16), pltpu.SemaphoreType.DMA((7,))],
        compiler_params=pltpu.CompilerParams(vmem_limit_bytes=16 << 20),
        name="expand",
    )(first, middle, last, idx)


def shards(diag_jac, xface_jac, side_jac, orient, owner):
    tabs = tables()
    anys = pl.BlockSpec(memory_space=ANY)
    sds = jax.ShapeDtypeStruct
    dma = pltpu.SemaphoreType.DMA
    pieces = pl.pallas_call(
        project_and_send,
        out_shape=(sds((GRP, 2, FIRST), BF16), sds((GRP, 2, MIDDLE), BF16), sds((GRP, 2, DIAG), BF16)),
        in_specs=[pl.BlockSpec(memory_space=pltpu.HBM)] * 10,
        out_specs=(anys, anys, anys),
        scratch_shapes=[pltpu.SMEM((ELEMS,), jnp.int32), pltpu.SMEM((ELEMS,), jnp.int32),
                        pltpu.VMEM((ELEMS, 2, FLAT), BF16), pltpu.VMEM((ELEMS, 4, FLAT), BF16),
                        pltpu.VMEM((ELEMS, NF, NF), BF16)]
        + [pltpu.VMEM(t.shape, BF16) for t in tabs]
        + [pltpu.VMEM((ROWS, 16000), BF16), pltpu.VMEM((ROWS, ZT * LANE), F32),
           pltpu.VMEM((NV * 2 * ROWS, 512), BF16), pltpu.VMEM((2, 80 * GROUP, NF), BF16), pltpu.VMEM((480, LANE), F32),
           pltpu.VMEM((16, DIAG), F32), pltpu.VMEM((16, TILED), BF16), pltpu.VMEM((16, TILED), BF16),
           pltpu.VMEM((OWNERS, 2, FIRST), BF16), pltpu.VMEM((OWNERS, 2, MIDDLE), BF16), pltpu.VMEM((OWNERS, 2, DIAG), BF16),
           dma((21,)), dma((3,)), dma, dma, dma((OWNERS,)), dma((GRP,)), dma((OWNERS,)), dma((GRP,)),
           dma((OWNERS,)), dma((GRP,))],
        compiler_params=pltpu.CompilerParams(collective_id=0, has_side_effects=True, vmem_limit_bytes=40 << 20),
        name="project_and_send",
    )(*[pltpu.with_memory_space_constraint(a, pltpu.HBM)
        for a in (orient, owner, xface_jac, side_jac, diag_jac, *tabs)])
    planes = call_expand(*pieces)
    return jnp.transpose(planes, (1, 0, 2))


def solution(mesh):
    split_all = P(("slab", "grp"), None, None)
    vector = P(("slab", "grp"))
    return jax.shard_map(shards, mesh=mesh, in_specs=(split_all, split_all, split_all, vector, vector),
                         out_specs=split_all, check_vma=False)
```

```python
import functools
import jax
import jax.numpy as jnp
import numpy as np
from jax import lax
from jax.experimental import pallas as pl
from jax.experimental.pallas import tpu as pltpu
from jax.sharding import PartitionSpec as P

NV = 5
MESH = pl.DeviceIdType.MESH
ANY = pl.ANY
F32 = jnp.float32
BF16 = jnp.bfloat16
LANE = 128
ELEMS = 12
NF = 625
FLAT = 15625
ROWS = 80
ZT = 20
TILED = NV * LANE
FACE = 400
DIAG = 13 * LANE
TURNS = ([0, 1, 2, 3], [2, 0, 3, 1], [3, 2, 1, 0], [1, 3, 0, 2])


def gll_points(degree):
    if degree == 1:
        return np.array([-1.0, 1.0])
    if degree == 2:
        return np.array([-1.0, 0.0, 1.0])
    inner_pt = np.sqrt(3.0 / 7.0)
    return np.array([-1.0, -inner_pt, 0.0, inner_pt, 1.0])


def lagrange(source_deg, target_deg):
    source = gll_points(source_deg)
    target = gll_points(target_deg)
    result = np.ones((target_deg + 1, source_deg + 1))
    for j in range(source_deg + 1):
        for m in range(source_deg + 1):
            if m != j:
                result[:, j] = result[:, j] * (target - source[m]) / (source[j] - source[m])
    return result


def split(table):
    lead = table.astype(BF16).astype(np.float64)
    return lead, (table - lead).astype(BF16).astype(np.float64)


def tables():
    line = lagrange(2, 4) @ lagrange(1, 2)
    face = np.kron(line, line)
    wide = np.kron(np.eye(32), face)
    wb = np.zeros((992, 256))
    for part, table in enumerate(split(wide)):
        wb[96:896, part * LANE:(part + 1) * LANE] = table
    w2 = np.zeros((512, 256))
    for part, table in enumerate(split(np.kron(face, np.eye(20)))):
        w2[:500, part * LANE:part * LANE + 80] = table
    turn = np.zeros((LANE, 6 * LANE))
    for o in (1, 2, 3):
        for jj in range(4):
            for v in range(NV):
                for kk in range(4):
                    lane = jj * 20 + v * 4 + kk
                    turn[jj * 20 + v * 4 + TURNS[o][kk], (o - 1) * LANE + lane] = 1
                    turn[TURNS[o][jj] * 20 + v * 4 + kk, (o + 2) * LANE + lane] = 1
    cube = np.kron(np.eye(NV), np.kron(np.kron(line, line), line))
    lead, rest = split(cube)
    right = np.zeros((NF, 2 * LANE))
    right[:, :40] = lead
    right[:, LANE:LANE + 40] = rest
    left = np.concatenate([lead.T, rest.T], axis=0)
    return [jnp.asarray(t.astype(BF16)) for t in (wb, w2, turn, right, left)]


def dot(a, b):
    return jnp.dot(a, b, preferred_element_type=F32)


def halves(value):
    lead = value.astype(BF16)
    return lead, (value - lead.astype(F32)).astype(BF16)


def iota(shape, dim):
    return lax.broadcasted_iota(jnp.int32, shape, dim)


def face_rows(x_ref, s_ref, wb_ref, w2_copy, w2_ref, xs, zf, zz):
    xs[0:24, 0:FLAT] = x_ref[...].reshape(24, FLAT)
    xs[32:80, 0:FLAT] = s_ref[...].reshape(48, FLAT)
    xs[24:32, :] = jnp.zeros((8, xs.shape[1]), BF16)
    xs[:, FLAT:] = jnp.zeros((ROWS, xs.shape[1] - FLAT), BF16)
    for q in range(4):
        tiles = range(q, ZT, 4)
        starts = [(800 * j) // LANE * LANE for j in tiles]
        rows = jnp.concatenate([xs[:, s:s + 896] for s in starts], axis=0)
        prod = dot(rows, wb_ref[96 - 32 * q:992 - 32 * q, :])
        for i, j in enumerate(tiles):
            part = prod[ROWS * i:ROWS * (i + 1)]
            zf[:, LANE * j:LANE * (j + 1)] = part[:, :LANE] + part[:, LANE:]
    lane = iota((ROWS, LANE), 1)
    for v in range(NV):
        first, off = divmod(500 * v, LANE)
        parts = [zf[:, LANE * (first + i):LANE * (first + i + 1)] for i in range(5 if off else 4)]
        if off:
            parts = [pltpu.roll(p, LANE - off, 1) for p in parts]
            parts = [jnp.where(lane < LANE - off, parts[i], parts[i + 1]) for i in range(4)]
        for i in range(4):
            lead, rest = halves(parts[i])
            at = 2 * ROWS * v
            zz[at:at + ROWS, LANE * i:LANE * (i + 1)] = lead
            zz[at + ROWS:at + 2 * ROWS, LANE * i:LANE * (i + 1)] = rest
    w2_copy.wait()
    prod = dot(zz[...], w2_ref[...])
    out = []
    for v in range(NV):
        lead, rest = prod[2 * ROWS * v:2 * ROWS * v + ROWS], prod[2 * ROWS * v + ROWS:2 * ROWS * (v + 1)]
        out.append(lead[:, :LANE] + lead[:, LANE:] + rest[:, :LANE])
    return out


def packed(placed, kinds):
    lane = iota((16, LANE), 1)
    tiles = [None] * (-(-FACE * kinds // LANE))
    for k in range(kinds):
        for v in range(NV):
            value = placed[16 * k:16 * k + 16, LANE * v:LANE * (v + 1)]
            at, shift = divmod(FACE * k + 80 * v, LANE)
            if shift:
                value = pltpu.roll(value, shift, 1)
            tiles[at] = value if shift == 0 else jnp.where(lane >= shift, value, tiles[at])
            if shift + 80 > LANE:
                tiles[at + 1] = value
    return jnp.concatenate(tiles, axis=1)


def turned(out, turn_ref, orient_ref):
    x = jnp.concatenate([t[0:32].astype(BF16) for t in out], axis=0)
    prod = dot(x, turn_ref[...])
    row = lax.rem(iota((NV * 32, LANE), 0), 32)
    o = jnp.zeros((NV * 32, LANE), jnp.int32)
    for e in range(ELEMS):
        o = jnp.where(row // 2 == e, orient_ref[e], o)
    odd = lax.rem(row, 2)
    result = x.astype(F32)
    for k in (1, 2, 3):
        result = jnp.where((o == k) & (odd == 0), prod[:, (k - 1) * LANE:k * LANE], result)
        result = jnp.where((o == k) & (odd == 1), prod[:, (k + 2) * LANE:(k + 3) * LANE], result)
    result = result.astype(BF16)
    return jnp.concatenate([result[32 * v:32 * v + 32] for v in range(NV)], axis=1)


def placement(owner_ref):
    lane = iota((16, LANE), 1)
    sub = iota((16, LANE), 0)
    on_lane = jnp.full((16, LANE), -1, jnp.int32)
    on_sub = jnp.full((16, LANE), -2, jnp.int32)
    for e in range(ELEMS):
        on_lane = jnp.where(lane == e, owner_ref[e], on_lane)
        on_sub = jnp.where(sub == e, owner_ref[e], on_sub)
    same = jnp.where((on_lane == on_sub) & (sub < lane), 1, 0)
    rank = jnp.sum(same, axis=0, keepdims=True)
    dest = jnp.where(lane < ELEMS, 2 * on_lane + rank, -1)
    return jnp.where(dest == sub, 1.0, 0.0).astype(F32)


def diag_left(e, dv, left_ref, hs, slot, i):
    prod = dot(left_ref[...], dv[e])
    lead, rest = halves(prod[0:40] + prod[40:80])
    hs[slot, 80 * i:80 * i + 40, :] = lead
    hs[slot, 80 * i + 40:80 * i + 80, :] = rest


def diag_right(first, count, hs, slot, right_ref, gs):
    prod = dot(hs[slot], right_ref[...])
    for i in range(count):
        lead, rest = prod[80 * i:80 * i + 40], prod[80 * i + 40:80 * i + 80]
        e = first + i
        gs[40 * e:40 * e + 40, :] = lead[:, :LANE] + lead[:, LANE:] + rest[:, :LANE]


def diag_rows(gs, first):
    lane = iota((6, LANE), 1)
    tiles = [jnp.zeros((6, LANE), F32) for _ in range(13)]
    for c in range(40):
        row = gs[pl.ds(40 * first + c, 6, stride=40), :]
        at, shift = divmod(40 * c, LANE)
        if shift:
            row = pltpu.roll(row, shift, 1)
        tiles[at] = jnp.where((lane >= shift) & (lane < shift + 40), row, tiles[at])
        if shift + 40 > LANE:
            tiles[at + 1] = jnp.where(lane < shift + 40 - LANE, row, tiles[at + 1])
    return jnp.concatenate(tiles, axis=1).astype(BF16)


GRP = 32
OWNERS = 8
SLOTS = 64
FIRST = 2048
MIDDLE = 512
GROUP = 3


def expand_tables():
    sel = [[4 * h + a for a in range(4)] for h in (0, 1)]
    sel += [[4 * a + 2 * h + b for a in (0, 1) for b in (0, 1)] for h in (0, 1)]
    sel += [[4 * a + 2 * b + h for a in (0, 1) for b in (0, 1)] for h in (0, 1)]
    ends = ((0, 1), (1, 0), (2, 3), (3, 2), (4, 5), (5, 4))
    rows, plan = [], []
    for k, (a, b) in enumerate(ends):
        source = np.full(13 * LANE, -1)
        for n in range(1600):
            c, d = divmod(n, 40)
            if c % 8 in sel[a] and d % 8 in sel[b]:
                source[n] = (FACE * max(k - 1, 0) + c // 8 * 80 + sel[a].index(c % 8) * 20
                             + d // 8 * 4 + sel[b].index(d % 8))
        for u in range(13):
            part = source[LANE * u:LANE * (u + 1)]
            for tile in sorted(set(part[part >= 0] // LANE)):
                plan.append((k, u, int(tile), len(rows)))
                rows.append(np.where(part // LANE == tile, part % LANE, -1))
    rows += [np.full(LANE, -1)] * (-len(rows) % 8)
    return plan, jnp.asarray(np.stack(rows).astype(np.int32))


def expand_block(plan, k, source, idx_ref, store):
    for u in range(13):
        value = jnp.zeros((SLOTS, LANE), F32)
        for _, _, tile, row in [p for p in plan if p[:2] == (k, u)]:
            idx = jnp.broadcast_to(idx_ref[row:row + 1, :], (SLOTS, LANE))
            part = source[:, LANE * tile:LANE * (tile + 1)].astype(F32)
            got = jnp.take_along_axis(part, jnp.maximum(idx, 0), axis=1, mode="promise_in_bounds")
            value = jnp.where(idx >= 0, got, value)
        width = min(LANE, 1600 - LANE * u)
        store(slice(LANE * u, LANE * u + width), value.astype(BF16)[:, :width])


def project_and_send(plan, orient_hbm, owner_hbm, x_hbm, s_hbm, d_hbm, wb_hbm, w2_hbm, tu_hbm, ri_hbm, le_hbm,
                     idx_hbm, planes_out, middle_out, last_out,
                     orient_ref, owner_ref, xv, sv, dv, wb, w2, tu, ri, le, xs, zf, zz, hs, gs, half, sent, minus,
                     first, middle, last, first_out, ov, idx_ref, sem, own_sem, plane_sem, step_send, step_recv,
                     first_send, first_recv, middle_send, middle_recv, last_send, last_recv):
    slab, grp = lax.axis_index("slab"), lax.axis_index("grp")
    slabs = lax.axis_size("slab")
    after, before = lax.rem(slab + 1, slabs), lax.rem(slab + slabs - 1, slabs)
    is_owner = grp < OWNERS

    pairs = [(x_hbm, xv), (s_hbm, sv), (wb_hbm, wb), (w2_hbm, w2), (tu_hbm, tu), (le_hbm, le), (ri_hbm, ri)]
    idx_copy = pltpu.make_async_copy(idx_hbm, idx_ref, sem.at[21])
    scalars = [pltpu.make_async_copy(orient_hbm, orient_ref, sem.at[19]), pltpu.make_async_copy(owner_hbm, owner_ref, sem.at[20])]
    copies = [pltpu.make_async_copy(a, b, sem.at[i]) for i, (a, b) in enumerate(pairs)]
    blocks = [pltpu.make_async_copy(d_hbm.at[e], dv.at[e], sem.at[7 + e]) for e in range(ELEMS)]
    for c in scalars + copies:
        c.start()

    barrier = pltpu.get_barrier_semaphore()
    pl.semaphore_signal(barrier, inc=1, device_id=(before, grp), device_id_type=MESH)

    @pl.when(is_owner)
    def _():
        def greet(i, carry):
            @pl.when(i != grp)
            def _():
                pl.semaphore_signal(barrier, inc=1, device_id=(slab, i), device_id_type=MESH)
            return carry
        lax.fori_loop(0, GRP, greet, 0)

    def to_owner(src, dst, send, recv, o):
        return pltpu.make_async_remote_copy(
            src_ref=src.at[o], dst_ref=dst.at[grp], send_sem=send.at[o], recv_sem=recv.at[grp],
            device_id=(slab, o), device_id_type=MESH)

    def keep(src, dst, i):
        return pltpu.make_async_copy(src.at[lax.rem(grp, OWNERS)], dst.at[grp], own_sem.at[i])

    def scatter(src, dst, send, recv, i):
        for k in range(1, OWNERS):
            to_owner(src, dst, send, recv, lax.rem(grp + k, OWNERS)).start()

        @pl.when(is_owner)
        def _():
            keep(src, dst, i).start()

        @pl.when(jnp.logical_not(is_owner))
        def _():
            to_owner(src, dst, send, recv, lax.rem(grp, OWNERS)).start()

    def sent_all(src, dst, send, recv):
        for k in range(1, OWNERS):
            to_owner(src, dst, send, recv, lax.rem(grp + k, OWNERS)).wait_send()

        @pl.when(jnp.logical_not(is_owner))
        def _():
            to_owner(src, dst, send, recv, lax.rem(grp, OWNERS)).wait_send()

    def arrived(src, dst, send, recv, i):
        keep(src, dst, i).wait()
        for k in range(1, GRP):
            pltpu.make_async_remote_copy(
                src_ref=src.at[0], dst_ref=dst.at[lax.rem(grp + k, GRP)], send_sem=send.at[0],
                recv_sem=recv.at[lax.rem(grp + k, GRP)], device_id=(slab, grp), device_id_type=MESH).wait_recv()

    for c in scalars:
        c.wait()
    place = placement(owner_ref)
    pb = place.astype(BF16)
    pb_late = pltpu.roll(place, LANE - 6, 1).astype(BF16)
    for c in copies[:3]:
        c.wait()
    for c in blocks + [idx_copy]:
        c.start()
    out = face_rows(xv, sv, wb, copies[3], w2, xs, zf, zz)
    copies[4].wait()
    x_rows = turned(out, tu, orient_ref)
    pick = jnp.where((iota((16, 32), 1) == 2 * iota((16, 32), 0) + 1) & (iota((16, 32), 0) < ELEMS), 1.0, 0.0)
    sent[...] = dot(pick.astype(BF16), x_rows).astype(BF16)

    @pl.when(is_owner)
    def _():
        pl.semaphore_wait(barrier, OWNERS)

    @pl.when(jnp.logical_not(is_owner))
    def _():
        pl.semaphore_wait(barrier, OWNERS + 1)

    step = pltpu.make_async_remote_copy(
        src_ref=sent, dst_ref=minus, send_sem=step_send, recv_sem=step_recv,
        device_id=(after, grp), device_id_type=MESH)
    step.start()

    side_rows = jnp.concatenate([t[32:80].astype(BF16) for t in out], axis=1)
    all_rows = jnp.concatenate([x_rows, side_rows], axis=0)
    rr, ee = iota((LANE, ROWS), 1), iota((LANE, ROWS), 0)
    picks = [jnp.where((rr == 2 * ee) & (ee < ELEMS), 1.0, 0.0)]
    picks += [jnp.where((rr == 32 + 4 * ee + f) & (ee < ELEMS), 1.0, 0.0) for f in range(4)]
    who = jnp.concatenate([dot(pb, p.astype(BF16)) for p in picks], axis=0).astype(BF16)
    first[...] = packed(dot(who, all_rows), 5).astype(BF16).reshape(OWNERS, 2, FIRST)
    scatter(first, first_out, first_send, first_recv, 0)

    copies[5].wait()
    copies[6].wait()
    groups = ELEMS // GROUP
    for t in range(groups + 1):
        if t < groups:
            for i in range(GROUP):
                blocks[GROUP * t + i].wait()
            for i in range(GROUP):
                diag_left(GROUP * t + i, dv, le, hs, t % 2, i)
        if t > 0:
            diag_right(GROUP * (t - 1), GROUP, hs, (t - 1) % 2, ri, gs)
        if GROUP * t == 6:
            half[...] = dot(pb[:, :6], diag_rows(gs, 0))
    placed = half[...] + dot(pb_late[:, :6], diag_rows(gs, 6))
    last[...] = placed.astype(BF16).reshape(OWNERS, 2, DIAG)
    scatter(last, last_out, last_send, last_recv, 2)
    step.wait()
    placed = dot(pb[:, :16], minus[...])
    middle[...] = packed(placed, 1).astype(BF16).reshape(OWNERS, 2, MIDDLE)
    scatter(middle, middle_out, middle_send, middle_recv, 1)
    planes = [pltpu.make_async_copy(ov.at[k], planes_out.at[k], plane_sem.at[k]) for k in range(5)]
    idx_copy.wait()

    @pl.when(jnp.logical_not(is_owner))
    def _():
        for k in range(5):
            ov[k] = jnp.zeros((SLOTS, 1600), BF16)
            planes[k].start()

    @pl.when(is_owner)
    def _():
        arrived(first, first_out, first_send, first_recv, 0)
        source = first_out[...].reshape(SLOTS, FIRST)
        for k in range(5):
            def store(at, value, k=k):
                ov[k, :, at] = value
            expand_block(plan, k + 1, source, idx_ref, store)
            planes[k].start()

    sent_all(first, first_out, first_send, first_recv)
    sent_all(middle, middle_out, middle_send, middle_recv)
    sent_all(last, last_out, last_send, last_recv)
    for p in planes:
        p.wait()

    @pl.when(is_owner)
    def _():
        arrived(middle, middle_out, middle_send, middle_recv, 1)
        arrived(last, last_out, last_send, last_recv, 2)


def expand(plan, planes_ref, middle_ref, last_ref, idx_ref, out_hbm, ov, sem):
    owner = lax.axis_index("grp") < OWNERS
    copies = [pltpu.make_async_copy(ov.at[k], out_hbm.at[k], sem.at[k]) for k in range(2)]
    copies += [pltpu.make_async_copy(planes_ref.at[k - 2], out_hbm.at[k], sem.at[k]) for k in range(2, 7)]
    for c in copies[2:]:
        c.start()

    @pl.when(jnp.logical_not(owner))
    def _():
        for k in range(2):
            ov[k] = jnp.zeros((SLOTS, 1600), BF16)
            copies[k].start()

    @pl.when(owner)
    def _():
        ov[0] = last_ref[...].reshape(SLOTS, DIAG)[:, :1600]
        copies[0].start()

        def store(at, value):
            ov[1, :, at] = value
        expand_block(plan, 0, middle_ref[...].reshape(SLOTS, MIDDLE), idx_ref, store)
        copies[1].start()

    for c in copies:
        c.wait()


def shards(diag_jac, xface_jac, side_jac, orient, owner):
    tabs = tables()
    plan, idx = expand_tables()
    anys = pl.BlockSpec(memory_space=ANY)
    vm = pl.BlockSpec(memory_space=pltpu.VMEM)
    hbm = pl.BlockSpec(memory_space=pltpu.HBM)
    sds = jax.ShapeDtypeStruct
    dma = pltpu.SemaphoreType.DMA
    planes, middle, last = pl.pallas_call(
        functools.partial(project_and_send, plan),
        out_shape=(sds((5, SLOTS, 1600), BF16), sds((GRP, 2, MIDDLE), BF16), sds((GRP, 2, DIAG), BF16)),
        in_specs=[hbm] * 11,
        out_specs=(anys, anys, anys),
        scratch_shapes=[pltpu.SMEM((ELEMS,), jnp.int32), pltpu.SMEM((ELEMS,), jnp.int32),
                        pltpu.VMEM((ELEMS, 2, FLAT), BF16), pltpu.VMEM((ELEMS, 4, FLAT), BF16),
                        pltpu.VMEM((ELEMS, NF, NF), BF16)]
        + [pltpu.VMEM(t.shape, BF16) for t in tabs]
        + [pltpu.VMEM((ROWS, 16000), BF16), pltpu.VMEM((ROWS, ZT * LANE), F32),
           pltpu.VMEM((NV * 2 * ROWS, 512), BF16), pltpu.VMEM((2, 80 * GROUP, NF), BF16), pltpu.VMEM((480, LANE), F32),
           pltpu.VMEM((16, DIAG), F32), pltpu.VMEM((16, TILED), BF16), pltpu.VMEM((16, TILED), BF16),
           pltpu.VMEM((OWNERS, 2, FIRST), BF16), pltpu.VMEM((OWNERS, 2, MIDDLE), BF16), pltpu.VMEM((OWNERS, 2, DIAG), BF16),
           pltpu.VMEM((GRP, 2, FIRST), BF16), pltpu.VMEM((5, SLOTS, 1600), BF16), pltpu.VMEM(idx.shape, jnp.int32),
           dma((22,)), dma((3,)), dma((5,)), dma, dma, dma((OWNERS,)), dma((GRP,)), dma((OWNERS,)), dma((GRP,)),
           dma((OWNERS,)), dma((GRP,))],
        compiler_params=pltpu.CompilerParams(collective_id=0, has_side_effects=True, vmem_limit_bytes=40 << 20),
        name="project_and_send",
    )(*[pltpu.with_memory_space_constraint(a, pltpu.HBM)
        for a in (orient, owner, xface_jac, side_jac, diag_jac, *tabs, idx)])
    planes = pl.pallas_call(
        functools.partial(expand, plan),
        out_shape=sds((7, SLOTS, 1600), BF16),
        in_specs=[vm, vm, vm, vm],
        out_specs=hbm,
        scratch_shapes=[pltpu.VMEM((2, SLOTS, 1600), BF16), dma((7,))],
        compiler_params=pltpu.CompilerParams(vmem_limit_bytes=16 << 20),
        name="expand",
    )(planes, middle, last, idx)
    return jnp.transpose(planes, (1, 0, 2))


def solution(mesh):
    split_all = P(("slab", "grp"), None, None)
    vector = P(("slab", "grp"))
    return jax.shard_map(shards, mesh=mesh, in_specs=(split_all, split_all, split_all, vector, vector),
                         out_specs=split_all, check_vma=False)
```

```python
import functools
import jax
import jax.numpy as jnp
import numpy as np
from jax import lax
from jax.experimental import pallas as pl
from jax.experimental.pallas import tpu as pltpu
from jax.sharding import PartitionSpec as P

NV = 5
MESH = pl.DeviceIdType.MESH
ANY = pl.ANY
F32 = jnp.float32
BF16 = jnp.bfloat16
LANE = 128
ELEMS = 12
NF = 625
FLAT = 15625
ROWS = 80
ZT = 20
TILED = NV * LANE
FACE = 400
DIAG = 13 * LANE
TURNS = ([0, 1, 2, 3], [2, 0, 3, 1], [3, 2, 1, 0], [1, 3, 0, 2])


def gll_points(degree):
    if degree == 1:
        return np.array([-1.0, 1.0])
    if degree == 2:
        return np.array([-1.0, 0.0, 1.0])
    inner_pt = np.sqrt(3.0 / 7.0)
    return np.array([-1.0, -inner_pt, 0.0, inner_pt, 1.0])


def lagrange(source_deg, target_deg):
    source = gll_points(source_deg)
    target = gll_points(target_deg)
    result = np.ones((target_deg + 1, source_deg + 1))
    for j in range(source_deg + 1):
        for m in range(source_deg + 1):
            if m != j:
                result[:, j] = result[:, j] * (target - source[m]) / (source[j] - source[m])
    return result


def split(table):
    lead = table.astype(BF16).astype(np.float64)
    return lead, (table - lead).astype(BF16).astype(np.float64)


def tables():
    line = lagrange(2, 4) @ lagrange(1, 2)
    face = np.kron(line, line)
    wide = np.kron(np.eye(32), face)
    wb = np.zeros((992, 256))
    for part, table in enumerate(split(wide)):
        wb[96:896, part * LANE:(part + 1) * LANE] = table
    w2 = np.zeros((512, 256))
    for part, table in enumerate(split(np.kron(face, np.eye(20)))):
        w2[:500, part * LANE:part * LANE + 80] = table
    turn = np.zeros((LANE, 6 * LANE))
    for o in (1, 2, 3):
        for jj in range(4):
            for v in range(NV):
                for kk in range(4):
                    lane = jj * 20 + v * 4 + kk
                    turn[jj * 20 + v * 4 + TURNS[o][kk], (o - 1) * LANE + lane] = 1
                    turn[TURNS[o][jj] * 20 + v * 4 + kk, (o + 2) * LANE + lane] = 1
    cube = np.kron(np.eye(NV), np.kron(np.kron(line, line), line))
    lead, rest = split(cube)
    right = np.zeros((NF, 2 * LANE))
    right[:, :40] = lead
    right[:, LANE:LANE + 40] = rest
    left = np.concatenate([lead.T, rest.T], axis=0)
    return [jnp.asarray(t.astype(BF16)) for t in (wb, w2, turn, right, left)]


def dot(a, b):
    return jnp.dot(a, b, preferred_element_type=F32)


def halves(value):
    lead = value.astype(BF16)
    return lead, (value - lead.astype(F32)).astype(BF16)


def iota(shape, dim):
    return lax.broadcasted_iota(jnp.int32, shape, dim)


def face_rows(x_ref, s_ref, wb_ref, w2_copy, w2_ref, xs, zf, zz):
    xs[0:24, 0:FLAT] = x_ref[...].reshape(24, FLAT)
    xs[32:80, 0:FLAT] = s_ref[...].reshape(48, FLAT)
    xs[24:32, :] = jnp.zeros((8, xs.shape[1]), BF16)
    xs[:, FLAT:] = jnp.zeros((ROWS, xs.shape[1] - FLAT), BF16)
    for q in range(4):
        tiles = range(q, ZT, 4)
        starts = [(800 * j) // LANE * LANE for j in tiles]
        rows = jnp.concatenate([xs[:, s:s + 896] for s in starts], axis=0)
        prod = dot(rows, wb_ref[96 - 32 * q:992 - 32 * q, :])
        for i, j in enumerate(tiles):
            part = prod[ROWS * i:ROWS * (i + 1)]
            zf[:, LANE * j:LANE * (j + 1)] = part[:, :LANE] + part[:, LANE:]
    lane = iota((ROWS, LANE), 1)
    for v in range(NV):
        first, off = divmod(500 * v, LANE)
        parts = [zf[:, LANE * (first + i):LANE * (first + i + 1)] for i in range(5 if off else 4)]
        if off:
            parts = [pltpu.roll(p, LANE - off, 1) for p in parts]
            parts = [jnp.where(lane < LANE - off, parts[i], parts[i + 1]) for i in range(4)]
        for i in range(4):
            lead, rest = halves(parts[i])
            at = 2 * ROWS * v
            zz[at:at + ROWS, LANE * i:LANE * (i + 1)] = lead
            zz[at + ROWS:at + 2 * ROWS, LANE * i:LANE * (i + 1)] = rest
    w2_copy.wait()
    prod = dot(zz[...], w2_ref[...])
    out = []
    for v in range(NV):
        lead, rest = prod[2 * ROWS * v:2 * ROWS * v + ROWS], prod[2 * ROWS * v + ROWS:2 * ROWS * (v + 1)]
        out.append(lead[:, :LANE] + lead[:, LANE:] + rest[:, :LANE])
    return out


def packed(placed, kinds):
    lane = iota((16, LANE), 1)
    tiles = [None] * (-(-FACE * kinds // LANE))
    for k in range(kinds):
        for v in range(NV):
            value = placed[16 * k:16 * k + 16, LANE * v:LANE * (v + 1)]
            at, shift = divmod(FACE * k + 80 * v, LANE)
            if shift:
                value = pltpu.roll(value, shift, 1)
            tiles[at] = value if shift == 0 else jnp.where(lane >= shift, value, tiles[at])
            if shift + 80 > LANE:
                tiles[at + 1] = value
    return jnp.concatenate(tiles, axis=1)


def turned(out, turn_ref, orient_ref):
    x = jnp.concatenate([t[0:32].astype(BF16) for t in out], axis=0)
    prod = dot(x, turn_ref[...])
    row = lax.rem(iota((NV * 32, LANE), 0), 32)
    o = jnp.zeros((NV * 32, LANE), jnp.int32)
    for e in range(ELEMS):
        o = jnp.where(row // 2 == e, orient_ref[e], o)
    odd = lax.rem(row, 2)
    result = x.astype(F32)
    for k in (1, 2, 3):
        result = jnp.where((o == k) & (odd == 0), prod[:, (k - 1) * LANE:k * LANE], result)
        result = jnp.where((o == k) & (odd == 1), prod[:, (k + 2) * LANE:(k + 3) * LANE], result)
    result = result.astype(BF16)
    return jnp.concatenate([result[32 * v:32 * v + 32] for v in range(NV)], axis=1)


def placement(owner_ref):
    lane = iota((16, LANE), 1)
    sub = iota((16, LANE), 0)
    on_lane = jnp.full((16, LANE), -1, jnp.int32)
    on_sub = jnp.full((16, LANE), -2, jnp.int32)
    for e in range(ELEMS):
        on_lane = jnp.where(lane == e, owner_ref[e], on_lane)
        on_sub = jnp.where(sub == e, owner_ref[e], on_sub)
    same = jnp.where((on_lane == on_sub) & (sub < lane), 1, 0)
    rank = jnp.sum(same, axis=0, keepdims=True)
    dest = jnp.where(lane < ELEMS, 2 * on_lane + rank, -1)
    return jnp.where(dest == sub, 1.0, 0.0).astype(F32)


def diag_left(e, dv, left_ref, hs, slot, i):
    prod = dot(left_ref[...], dv[e])
    lead, rest = halves(prod[0:40] + prod[40:80])
    hs[slot, 80 * i:80 * i + 40, :] = lead
    hs[slot, 80 * i + 40:80 * i + 80, :] = rest


def diag_right(first, count, hs, slot, right_ref, gs):
    prod = dot(hs[slot], right_ref[...])
    for i in range(count):
        lead, rest = prod[80 * i:80 * i + 40], prod[80 * i + 40:80 * i + 80]
        e = first + i
        gs[40 * e:40 * e + 40, :] = lead[:, :LANE] + lead[:, LANE:] + rest[:, :LANE]


def diag_rows(gs, first):
    lane = iota((6, LANE), 1)
    tiles = [jnp.zeros((6, LANE), F32) for _ in range(13)]
    for c in range(40):
        row = gs[pl.ds(40 * first + c, 6, stride=40), :]
        at, shift = divmod(40 * c, LANE)
        if shift:
            row = pltpu.roll(row, shift, 1)
        tiles[at] = jnp.where((lane >= shift) & (lane < shift + 40), row, tiles[at])
        if shift + 40 > LANE:
            tiles[at + 1] = jnp.where(lane < shift + 40 - LANE, row, tiles[at + 1])
    return jnp.concatenate(tiles, axis=1).astype(BF16)


GRP = 32
OWNERS = 8
SLOTS = 64
FIRST = 2048
MINUS = 512
LAST = MINUS + DIAG
GROUP = 3


def expand_tables():
    sel = [[4 * h + a for a in range(4)] for h in (0, 1)]
    sel += [[4 * a + 2 * h + b for a in (0, 1) for b in (0, 1)] for h in (0, 1)]
    sel += [[4 * a + 2 * b + h for a in (0, 1) for b in (0, 1)] for h in (0, 1)]
    ends = ((0, 1), (1, 0), (2, 3), (3, 2), (4, 5), (5, 4))
    rows, plan = [], []
    for k, (a, b) in enumerate(ends):
        source = np.full(13 * LANE, -1)
        for n in range(1600):
            c, d = divmod(n, 40)
            if c % 8 in sel[a] and d % 8 in sel[b]:
                source[n] = (FACE * max(k - 1, 0) + c // 8 * 80 + sel[a].index(c % 8) * 20
                             + d // 8 * 4 + sel[b].index(d % 8))
        for u in range(13):
            part = source[LANE * u:LANE * (u + 1)]
            for tile in sorted(set(part[part >= 0] // LANE)):
                plan.append((k, u, int(tile), len(rows)))
                rows.append(np.where(part // LANE == tile, part % LANE, -1))
    rows += [np.full(LANE, -1)] * (-len(rows) % 8)
    return plan, jnp.asarray(np.stack(rows).astype(np.int32))


def expand_block(plan, k, source, idx_ref, store):
    for u in range(13):
        value = jnp.zeros((SLOTS, LANE), F32)
        for _, _, tile, row in [p for p in plan if p[:2] == (k, u)]:
            idx = jnp.broadcast_to(idx_ref[row:row + 1, :], (SLOTS, LANE))
            part = source[:, LANE * tile:LANE * (tile + 1)].astype(F32)
            got = jnp.take_along_axis(part, jnp.maximum(idx, 0), axis=1, mode="promise_in_bounds")
            value = jnp.where(idx >= 0, got, value)
        width = min(LANE, 1600 - LANE * u)
        store(slice(LANE * u, LANE * u + width), value.astype(BF16)[:, :width])


def project_and_send(plan, orient_hbm, owner_hbm, x_hbm, s_hbm, d_hbm, wb_hbm, w2_hbm, tu_hbm, ri_hbm, le_hbm,
                     idx_hbm, planes_out, last_out,
                     orient_ref, owner_ref, xv, sv, dv, wb, w2, tu, ri, le, xs, zf, zz, hs, gs, half, sent, minus,
                     first, last, first_out, ov, idx_ref, sem, own_sem, plane_sem, step_send, step_recv,
                     first_send, first_recv, last_send, last_recv):
    slab, grp = lax.axis_index("slab"), lax.axis_index("grp")
    slabs = lax.axis_size("slab")
    after, before = lax.rem(slab + 1, slabs), lax.rem(slab + slabs - 1, slabs)
    is_owner = grp < OWNERS

    pairs = [(x_hbm, xv), (s_hbm, sv), (wb_hbm, wb), (w2_hbm, w2), (tu_hbm, tu), (le_hbm, le), (ri_hbm, ri)]
    idx_copy = pltpu.make_async_copy(idx_hbm, idx_ref, sem.at[21])
    scalars = [pltpu.make_async_copy(orient_hbm, orient_ref, sem.at[19]), pltpu.make_async_copy(owner_hbm, owner_ref, sem.at[20])]
    copies = [pltpu.make_async_copy(a, b, sem.at[i]) for i, (a, b) in enumerate(pairs)]
    blocks = [pltpu.make_async_copy(d_hbm.at[e], dv.at[e], sem.at[7 + e]) for e in range(ELEMS)]
    for c in scalars + copies[:4]:
        c.start()

    barrier = pltpu.get_barrier_semaphore()
    pl.semaphore_signal(barrier, inc=1, device_id=(before, grp), device_id_type=MESH)

    @pl.when(is_owner)
    def _():
        def greet(i, carry):
            @pl.when(i != grp)
            def _():
                pl.semaphore_signal(barrier, inc=1, device_id=(slab, i), device_id_type=MESH)
            return carry
        lax.fori_loop(0, GRP, greet, 0)

    def to_owner(src, dst, send, recv, o):
        return pltpu.make_async_remote_copy(
            src_ref=src.at[o], dst_ref=dst.at[grp], send_sem=send.at[o], recv_sem=recv.at[grp],
            device_id=(slab, o), device_id_type=MESH)

    def keep(src, dst, i):
        return pltpu.make_async_copy(src.at[lax.rem(grp, OWNERS)], dst.at[grp], own_sem.at[i])

    def nth(k):
        return jnp.where(is_owner & (grp <= k), k + 1, k)

    def scatter(src, dst, send, recv, i):
        for k in range(OWNERS - 1):
            to_owner(src, dst, send, recv, nth(k)).start()

        @pl.when(is_owner)
        def _():
            keep(src, dst, i).start()

        @pl.when(jnp.logical_not(is_owner))
        def _():
            to_owner(src, dst, send, recv, OWNERS - 1).start()

    def sent_all(src, dst, send, recv):
        for k in range(OWNERS - 1):
            to_owner(src, dst, send, recv, nth(k)).wait_send()

        @pl.when(jnp.logical_not(is_owner))
        def _():
            to_owner(src, dst, send, recv, OWNERS - 1).wait_send()

    def arrived(src, dst, send, recv, i):
        keep(src, dst, i).wait()
        for k in range(1, GRP):
            pltpu.make_async_remote_copy(
                src_ref=src.at[0], dst_ref=dst.at[lax.rem(grp + k, GRP)], send_sem=send.at[0],
                recv_sem=recv.at[lax.rem(grp + k, GRP)], device_id=(slab, grp), device_id_type=MESH).wait_recv()

    for c in scalars:
        c.wait()
    place = placement(owner_ref)
    pb = place.astype(BF16)
    pb_late = pltpu.roll(place, LANE - 6, 1).astype(BF16)
    for c in copies[:3]:
        c.wait()
    for c in copies[4:] + blocks + [idx_copy]:
        c.start()
    out = face_rows(xv, sv, wb, copies[3], w2, xs, zf, zz)
    copies[4].wait()
    x_rows = turned(out, tu, orient_ref)
    pick = jnp.where((iota((16, 32), 1) == 2 * iota((16, 32), 0) + 1) & (iota((16, 32), 0) < ELEMS), 1.0, 0.0)
    sent[...] = dot(pick.astype(BF16), x_rows).astype(BF16)

    @pl.when(is_owner)
    def _():
        pl.semaphore_wait(barrier, OWNERS)

    @pl.when(jnp.logical_not(is_owner))
    def _():
        pl.semaphore_wait(barrier, OWNERS + 1)

    step = pltpu.make_async_remote_copy(
        src_ref=sent, dst_ref=minus, send_sem=step_send, recv_sem=step_recv,
        device_id=(after, grp), device_id_type=MESH)
    step.start()

    side_rows = jnp.concatenate([t[32:80].astype(BF16) for t in out], axis=1)
    all_rows = jnp.concatenate([x_rows, side_rows], axis=0)
    rr, ee = iota((LANE, ROWS), 1), iota((LANE, ROWS), 0)
    picks = [jnp.where((rr == 2 * ee) & (ee < ELEMS), 1.0, 0.0)]
    picks += [jnp.where((rr == 32 + 4 * ee + f) & (ee < ELEMS), 1.0, 0.0) for f in range(4)]
    who = jnp.concatenate([dot(pb, p.astype(BF16)) for p in picks], axis=0).astype(BF16)
    first[...] = packed(dot(who, all_rows), 5).astype(BF16).reshape(OWNERS, 2, FIRST)
    scatter(first, first_out, first_send, first_recv, 0)

    copies[5].wait()
    copies[6].wait()
    groups = ELEMS // GROUP
    for t in range(groups + 1):
        if t < groups:
            for i in range(GROUP):
                blocks[GROUP * t + i].wait()
            for i in range(GROUP):
                diag_left(GROUP * t + i, dv, le, hs, t % 2, i)
        if t > 0:
            diag_right(GROUP * (t - 1), GROUP, hs, (t - 1) % 2, ri, gs)
        if GROUP * t == 6:
            half[...] = dot(pb[:, :6], diag_rows(gs, 0))
    placed = half[...] + dot(pb_late[:, :6], diag_rows(gs, 6))
    last[:, :, MINUS:] = placed.astype(BF16).reshape(OWNERS, 2, DIAG)
    step.wait()
    placed = dot(pb[:, :16], minus[...])
    last[:, :, :MINUS] = packed(placed, 1).astype(BF16).reshape(OWNERS, 2, MINUS)
    scatter(last, last_out, last_send, last_recv, 1)
    planes = [pltpu.make_async_copy(ov.at[k], planes_out.at[k], plane_sem.at[k]) for k in range(5)]
    idx_copy.wait()

    @pl.when(jnp.logical_not(is_owner))
    def _():
        for k in range(5):
            ov[k] = jnp.zeros((SLOTS, 1600), BF16)
            planes[k].start()

    @pl.when(is_owner)
    def _():
        arrived(first, first_out, first_send, first_recv, 0)
        source = first_out[...].reshape(SLOTS, FIRST)
        for k in range(5):
            def store(at, value, k=k):
                ov[k, :, at] = value
            expand_block(plan, k + 1, source, idx_ref, store)
            planes[k].start()

    sent_all(first, first_out, first_send, first_recv)
    sent_all(last, last_out, last_send, last_recv)
    for p in planes:
        p.wait()

    @pl.when(is_owner)
    def _():
        arrived(last, last_out, last_send, last_recv, 1)


def expand(plan, planes_ref, last_ref, idx_ref, out_hbm, ov, sem):
    owner = lax.axis_index("grp") < OWNERS
    copies = [pltpu.make_async_copy(ov.at[k], out_hbm.at[k], sem.at[k]) for k in range(2)]
    copies += [pltpu.make_async_copy(planes_ref.at[k - 2], out_hbm.at[k], sem.at[k]) for k in range(2, 7)]
    for c in copies[2:]:
        c.start()

    @pl.when(jnp.logical_not(owner))
    def _():
        for k in range(2):
            ov[k] = jnp.zeros((SLOTS, 1600), BF16)
            copies[k].start()

    @pl.when(owner)
    def _():
        ov[0] = last_ref[:, :, MINUS:].reshape(SLOTS, DIAG)[:, :1600]
        copies[0].start()

        def store(at, value):
            ov[1, :, at] = value
        expand_block(plan, 0, last_ref[:, :, :MINUS].reshape(SLOTS, MINUS), idx_ref, store)
        copies[1].start()

    for c in copies:
        c.wait()


def shards(diag_jac, xface_jac, side_jac, orient, owner):
    tabs = tables()
    plan, idx = expand_tables()
    anys = pl.BlockSpec(memory_space=ANY)
    vm = pl.BlockSpec(memory_space=pltpu.VMEM)
    hbm = pl.BlockSpec(memory_space=pltpu.HBM)
    sds = jax.ShapeDtypeStruct
    dma = pltpu.SemaphoreType.DMA
    planes, last = pl.pallas_call(
        functools.partial(project_and_send, plan),
        out_shape=(sds((5, SLOTS, 1600), BF16), sds((GRP, 2, LAST), BF16)),
        in_specs=[hbm] * 11,
        out_specs=(anys, anys),
        scratch_shapes=[pltpu.SMEM((ELEMS,), jnp.int32), pltpu.SMEM((ELEMS,), jnp.int32),
                        pltpu.VMEM((ELEMS, 2, FLAT), BF16), pltpu.VMEM((ELEMS, 4, FLAT), BF16),
                        pltpu.VMEM((ELEMS, NF, NF), BF16)]
        + [pltpu.VMEM(t.shape, BF16) for t in tabs]
        + [pltpu.VMEM((ROWS, 16000), BF16), pltpu.VMEM((ROWS, ZT * LANE), F32),
           pltpu.VMEM((NV * 2 * ROWS, 512), BF16), pltpu.VMEM((2, 80 * GROUP, NF), BF16), pltpu.VMEM((480, LANE), F32),
           pltpu.VMEM((16, DIAG), F32), pltpu.VMEM((16, TILED), BF16), pltpu.VMEM((16, TILED), BF16),
           pltpu.VMEM((OWNERS, 2, FIRST), BF16), pltpu.VMEM((OWNERS, 2, LAST), BF16),
           pltpu.VMEM((GRP, 2, FIRST), BF16), pltpu.VMEM((5, SLOTS, 1600), BF16), pltpu.VMEM(idx.shape, jnp.int32),
           dma((22,)), dma((2,)), dma((5,)), dma, dma, dma((OWNERS,)), dma((GRP,)), dma((OWNERS,)), dma((GRP,))],
        compiler_params=pltpu.CompilerParams(collective_id=0, has_side_effects=True, vmem_limit_bytes=40 << 20),
        name="project_and_send",
    )(*[pltpu.with_memory_space_constraint(a, pltpu.HBM)
        for a in (orient, owner, xface_jac, side_jac, diag_jac, *tabs, idx)])
    planes = pl.pallas_call(
        functools.partial(expand, plan),
        out_shape=sds((7, SLOTS, 1600), BF16),
        in_specs=[vm, vm, vm],
        out_specs=hbm,
        scratch_shapes=[pltpu.VMEM((2, SLOTS, 1600), BF16), dma((7,))],
        compiler_params=pltpu.CompilerParams(vmem_limit_bytes=16 << 20),
        name="expand",
    )(planes, last, idx)
    return jnp.transpose(planes, (1, 0, 2))


def solution(mesh):
    split_all = P(("slab", "grp"), None, None)
    vector = P(("slab", "grp"))
    return jax.shard_map(shards, mesh=mesh, in_specs=(split_all, split_all, split_all, vector, vector),
                         out_specs=split_all, check_vma=False)
```

```python
import functools
import jax
import jax.numpy as jnp
import numpy as np
from jax import lax
from jax.experimental import pallas as pl
from jax.experimental.pallas import tpu as pltpu
from jax.sharding import PartitionSpec as P

NV = 5
MESH = pl.DeviceIdType.MESH
ANY = pl.ANY
F32 = jnp.float32
BF16 = jnp.bfloat16
LANE = 128
ELEMS = 12
NF = 625
FLAT = 15625
ROWS = 80
ZT = 20
TILED = NV * LANE
FACE = 400
DIAG = 13 * LANE
TURNS = ([0, 1, 2, 3], [2, 0, 3, 1], [3, 2, 1, 0], [1, 3, 0, 2])


def gll_points(degree):
    if degree == 1:
        return np.array([-1.0, 1.0])
    if degree == 2:
        return np.array([-1.0, 0.0, 1.0])
    inner_pt = np.sqrt(3.0 / 7.0)
    return np.array([-1.0, -inner_pt, 0.0, inner_pt, 1.0])


def lagrange(source_deg, target_deg):
    source = gll_points(source_deg)
    target = gll_points(target_deg)
    result = np.ones((target_deg + 1, source_deg + 1))
    for j in range(source_deg + 1):
        for m in range(source_deg + 1):
            if m != j:
                result[:, j] = result[:, j] * (target - source[m]) / (source[j] - source[m])
    return result


def split(table):
    lead = table.astype(BF16).astype(np.float64)
    return lead, (table - lead).astype(BF16).astype(np.float64)


def tables():
    line = lagrange(2, 4) @ lagrange(1, 2)
    face = np.kron(line, line)
    wide = np.kron(np.eye(32), face)
    wb = np.zeros((992, 256))
    for part, table in enumerate(split(wide)):
        wb[96:896, part * LANE:(part + 1) * LANE] = table
    w2 = np.zeros((512, 256))
    for part, table in enumerate(split(np.kron(face, np.eye(20)))):
        w2[:500, part * LANE:part * LANE + 80] = table
    turn = np.zeros((LANE, 6 * LANE))
    for o in (1, 2, 3):
        for jj in range(4):
            for v in range(NV):
                for kk in range(4):
                    lane = jj * 20 + v * 4 + kk
                    turn[jj * 20 + v * 4 + TURNS[o][kk], (o - 1) * LANE + lane] = 1
                    turn[TURNS[o][jj] * 20 + v * 4 + kk, (o + 2) * LANE + lane] = 1
    cube = np.kron(np.eye(NV), np.kron(np.kron(line, line), line))
    lead, rest = split(cube)
    right = np.zeros((NF, 2 * LANE))
    right[:, :40] = lead
    right[:, LANE:LANE + 40] = rest
    left = np.concatenate([lead.T, rest.T], axis=0)
    return [jnp.asarray(t.astype(BF16)) for t in (wb, w2, turn, right, left)]


def dot(a, b):
    return jnp.dot(a, b, preferred_element_type=F32)


def halves(value):
    lead = value.astype(BF16)
    return lead, (value - lead.astype(F32)).astype(BF16)


def iota(shape, dim):
    return lax.broadcasted_iota(jnp.int32, shape, dim)


def face_rows(x_ref, s_ref, wb_ref, w2_copy, w2_ref, xs, zf, zz):
    xs[0:24, 0:FLAT] = x_ref[...].reshape(24, FLAT)
    xs[32:80, 0:FLAT] = s_ref[...].reshape(48, FLAT)
    xs[24:32, :] = jnp.zeros((8, xs.shape[1]), BF16)
    xs[:, FLAT:] = jnp.zeros((ROWS, xs.shape[1] - FLAT), BF16)
    for q in range(4):
        tiles = range(q, ZT, 4)
        starts = [(800 * j) // LANE * LANE for j in tiles]
        rows = jnp.concatenate([xs[:, s:s + 896] for s in starts], axis=0)
        prod = dot(rows, wb_ref[96 - 32 * q:992 - 32 * q, :])
        for i, j in enumerate(tiles):
            part = prod[ROWS * i:ROWS * (i + 1)]
            zf[:, LANE * j:LANE * (j + 1)] = part[:, :LANE] + part[:, LANE:]
    lane = iota((ROWS, LANE), 1)
    for v in range(NV):
        first, off = divmod(500 * v, LANE)
        parts = [zf[:, LANE * (first + i):LANE * (first + i + 1)] for i in range(5 if off else 4)]
        if off:
            parts = [pltpu.roll(p, LANE - off, 1) for p in parts]
            parts = [jnp.where(lane < LANE - off, parts[i], parts[i + 1]) for i in range(4)]
        for i in range(4):
            lead, rest = halves(parts[i])
            at = 2 * ROWS * v
            zz[at:at + ROWS, LANE * i:LANE * (i + 1)] = lead
            zz[at + ROWS:at + 2 * ROWS, LANE * i:LANE * (i + 1)] = rest
    w2_copy.wait()
    prod = dot(zz[...], w2_ref[...])
    out = []
    for v in range(NV):
        lead, rest = prod[2 * ROWS * v:2 * ROWS * v + ROWS], prod[2 * ROWS * v + ROWS:2 * ROWS * (v + 1)]
        out.append(lead[:, :LANE] + lead[:, LANE:] + rest[:, :LANE])
    return out


def packed(placed, kinds, start=0):
    lane = iota((16, LANE), 1)
    tiles = [jnp.zeros((16, LANE), F32)] * (-(-(start + FACE * kinds) // LANE))
    for k in range(kinds):
        for v in range(NV):
            value = placed[16 * k:16 * k + 16, LANE * v:LANE * (v + 1)]
            at, shift = divmod(start + FACE * k + 80 * v, LANE)
            if shift:
                value = pltpu.roll(value, shift, 1)
            tiles[at] = value if shift == 0 else jnp.where(lane >= shift, value, tiles[at])
            if shift + 80 > LANE:
                tiles[at + 1] = value
    return jnp.concatenate(tiles, axis=1)


def turned(out, turn_ref, orient_ref):
    x = jnp.concatenate([t[0:32].astype(BF16) for t in out], axis=0)
    prod = dot(x, turn_ref[...])
    row = lax.rem(iota((NV * 32, LANE), 0), 32)
    o = jnp.zeros((NV * 32, LANE), jnp.int32)
    for e in range(ELEMS):
        o = jnp.where(row // 2 == e, orient_ref[e], o)
    odd = lax.rem(row, 2)
    result = x.astype(F32)
    for k in (1, 2, 3):
        result = jnp.where((o == k) & (odd == 0), prod[:, (k - 1) * LANE:k * LANE], result)
        result = jnp.where((o == k) & (odd == 1), prod[:, (k + 2) * LANE:(k + 3) * LANE], result)
    result = result.astype(BF16)
    return jnp.concatenate([result[32 * v:32 * v + 32] for v in range(NV)], axis=1)


def placement(owner_ref):
    lane = iota((16, LANE), 1)
    sub = iota((16, LANE), 0)
    on_lane = jnp.full((16, LANE), -1, jnp.int32)
    on_sub = jnp.full((16, LANE), -2, jnp.int32)
    for e in range(ELEMS):
        on_lane = jnp.where(lane == e, owner_ref[e], on_lane)
        on_sub = jnp.where(sub == e, owner_ref[e], on_sub)
    same = jnp.where((on_lane == on_sub) & (sub < lane), 1, 0)
    rank = jnp.sum(same, axis=0, keepdims=True)
    dest = jnp.where(lane < ELEMS, 2 * on_lane + rank, -1)
    return jnp.where(dest == sub, 1.0, 0.0).astype(F32)


def diag_left(e, dv, left_ref, hs, slot, i):
    prod = dot(left_ref[...], dv[e])
    lead, rest = halves(prod[0:40] + prod[40:80])
    hs[slot, 80 * i:80 * i + 40, :] = lead
    hs[slot, 80 * i + 40:80 * i + 80, :] = rest


def diag_right(first, count, hs, slot, right_ref, gs):
    prod = dot(hs[slot], right_ref[...])
    for i in range(count):
        lead, rest = prod[80 * i:80 * i + 40], prod[80 * i + 40:80 * i + 80]
        e = first + i
        gs[40 * e:40 * e + 40, :] = lead[:, :LANE] + lead[:, LANE:] + rest[:, :LANE]


def diag_rows(gs, first):
    lane = iota((6, LANE), 1)
    tiles = [jnp.zeros((6, LANE), F32) for _ in range(13)]
    for c in range(40):
        row = gs[pl.ds(40 * first + c, 6, stride=40), :]
        at, shift = divmod(40 * c, LANE)
        if shift:
            row = pltpu.roll(row, shift, 1)
        tiles[at] = jnp.where((lane >= shift) & (lane < shift + 40), row, tiles[at])
        if shift + 40 > LANE:
            tiles[at + 1] = jnp.where(lane < shift + 40 - LANE, row, tiles[at + 1])
    return jnp.concatenate(tiles, axis=1).astype(BF16)


GRP = 32
OWNERS = 8
SLOTS = 64
FIRST = 2048
MINUS = 512
SHARED = DIAG - LANE
LAST = SHARED + MINUS
GROUP = 3


def expand_tables():
    sel = [[4 * h + a for a in range(4)] for h in (0, 1)]
    sel += [[4 * a + 2 * h + b for a in (0, 1) for b in (0, 1)] for h in (0, 1)]
    sel += [[4 * a + 2 * b + h for a in (0, 1) for b in (0, 1)] for h in (0, 1)]
    ends = ((0, 1), (1, 0), (2, 3), (3, 2), (4, 5), (5, 4))
    rows, plan = [], []
    for k, (a, b) in enumerate(ends):
        source = np.full(13 * LANE, -1)
        for n in range(1600):
            c, d = divmod(n, 40)
            if c % 8 in sel[a] and d % 8 in sel[b]:
                source[n] = ((FACE * (k - 1) if k else 64) + c // 8 * 80 + sel[a].index(c % 8) * 20
                             + d // 8 * 4 + sel[b].index(d % 8))
        for u in range(13):
            part = source[LANE * u:LANE * (u + 1)]
            for tile in sorted(set(part[part >= 0] // LANE)):
                plan.append((k, u, int(tile), len(rows)))
                rows.append(np.where(part // LANE == tile, part % LANE, -1))
    rows += [np.full(LANE, -1)] * (-len(rows) % 8)
    return plan, jnp.asarray(np.stack(rows).astype(np.int32))


def expand_block(plan, k, source, idx_ref, store):
    for u in range(13):
        value = jnp.zeros((SLOTS, LANE), F32)
        for _, _, tile, row in [p for p in plan if p[:2] == (k, u)]:
            idx = jnp.broadcast_to(idx_ref[row:row + 1, :], (SLOTS, LANE))
            part = source[:, LANE * tile:LANE * (tile + 1)].astype(F32)
            got = jnp.take_along_axis(part, jnp.maximum(idx, 0), axis=1, mode="promise_in_bounds")
            value = jnp.where(idx >= 0, got, value)
        width = min(LANE, 1600 - LANE * u)
        store(slice(LANE * u, LANE * u + width), value.astype(BF16)[:, :width])


def project_and_send(plan, orient_hbm, owner_hbm, x_hbm, s_hbm, d_hbm, wb_hbm, w2_hbm, tu_hbm, ri_hbm, le_hbm,
                     idx_hbm, planes_out, last_out,
                     orient_ref, owner_ref, xv, sv, dv, wb, w2, tu, ri, le, xs, zf, zz, hs, gs, half, sent, minus,
                     first, last, first_out, ov, idx_ref, sem, own_sem, plane_sem, step_send, step_recv,
                     first_send, first_recv, last_send, last_recv):
    slab, grp = lax.axis_index("slab"), lax.axis_index("grp")
    slabs = lax.axis_size("slab")
    after, before = lax.rem(slab + 1, slabs), lax.rem(slab + slabs - 1, slabs)
    is_owner = grp < OWNERS

    pairs = [(x_hbm, xv), (s_hbm, sv), (wb_hbm, wb), (w2_hbm, w2), (tu_hbm, tu), (le_hbm, le), (ri_hbm, ri)]
    idx_copy = pltpu.make_async_copy(idx_hbm, idx_ref, sem.at[21])
    scalars = [pltpu.make_async_copy(orient_hbm, orient_ref, sem.at[19]), pltpu.make_async_copy(owner_hbm, owner_ref, sem.at[20])]
    copies = [pltpu.make_async_copy(a, b, sem.at[i]) for i, (a, b) in enumerate(pairs)]
    blocks = [pltpu.make_async_copy(d_hbm.at[e], dv.at[e], sem.at[7 + e]) for e in range(ELEMS)]
    for c in scalars + copies[:4]:
        c.start()

    barrier = pltpu.get_barrier_semaphore()
    pl.semaphore_signal(barrier, inc=1, device_id=(before, grp), device_id_type=MESH)

    @pl.when(is_owner)
    def _():
        def greet(i, carry):
            @pl.when(i != grp)
            def _():
                pl.semaphore_signal(barrier, inc=1, device_id=(slab, i), device_id_type=MESH)
            return carry
        lax.fori_loop(0, GRP, greet, 0)

    def to_owner(src, dst, send, recv, o):
        return pltpu.make_async_remote_copy(
            src_ref=src.at[o], dst_ref=dst.at[grp], send_sem=send.at[o], recv_sem=recv.at[grp],
            device_id=(slab, o), device_id_type=MESH)

    def keep(src, dst, i):
        return pltpu.make_async_copy(src.at[lax.rem(grp, OWNERS)], dst.at[grp], own_sem.at[i])

    def nth(k):
        return jnp.where(is_owner & (grp <= k), k + 1, k)

    def scatter(src, dst, send, recv, i):
        for k in range(OWNERS - 1):
            to_owner(src, dst, send, recv, nth(k)).start()

        @pl.when(is_owner)
        def _():
            keep(src, dst, i).start()

        @pl.when(jnp.logical_not(is_owner))
        def _():
            to_owner(src, dst, send, recv, OWNERS - 1).start()

    def sent_all(src, dst, send, recv):
        for k in range(OWNERS - 1):
            to_owner(src, dst, send, recv, nth(k)).wait_send()

        @pl.when(jnp.logical_not(is_owner))
        def _():
            to_owner(src, dst, send, recv, OWNERS - 1).wait_send()

    def arrived(src, dst, send, recv, i):
        keep(src, dst, i).wait()
        for k in range(1, GRP):
            pltpu.make_async_remote_copy(
                src_ref=src.at[0], dst_ref=dst.at[lax.rem(grp + k, GRP)], send_sem=send.at[0],
                recv_sem=recv.at[lax.rem(grp + k, GRP)], device_id=(slab, grp), device_id_type=MESH).wait_recv()

    for c in scalars:
        c.wait()
    place = placement(owner_ref)
    pb = place.astype(BF16)
    pb_late = pltpu.roll(place, LANE - 6, 1).astype(BF16)
    for c in copies[:3]:
        c.wait()
    for c in copies[4:] + blocks + [idx_copy]:
        c.start()
    out = face_rows(xv, sv, wb, copies[3], w2, xs, zf, zz)
    copies[4].wait()
    x_rows = turned(out, tu, orient_ref)
    pick = jnp.where((iota((16, 32), 1) == 2 * iota((16, 32), 0) + 1) & (iota((16, 32), 0) < ELEMS), 1.0, 0.0)
    sent[...] = dot(pick.astype(BF16), x_rows).astype(BF16)

    @pl.when(is_owner)
    def _():
        pl.semaphore_wait(barrier, OWNERS)

    @pl.when(jnp.logical_not(is_owner))
    def _():
        pl.semaphore_wait(barrier, OWNERS + 1)

    step = pltpu.make_async_remote_copy(
        src_ref=sent, dst_ref=minus, send_sem=step_send, recv_sem=step_recv,
        device_id=(after, grp), device_id_type=MESH)
    step.start()

    side_rows = jnp.concatenate([t[32:80].astype(BF16) for t in out], axis=1)
    all_rows = jnp.concatenate([x_rows, side_rows], axis=0)
    rr, ee = iota((LANE, ROWS), 1), iota((LANE, ROWS), 0)
    picks = [jnp.where((rr == 2 * ee) & (ee < ELEMS), 1.0, 0.0)]
    picks += [jnp.where((rr == 32 + 4 * ee + f) & (ee < ELEMS), 1.0, 0.0) for f in range(4)]
    who = jnp.concatenate([dot(pb, p.astype(BF16)) for p in picks], axis=0).astype(BF16)
    first[...] = packed(dot(who, all_rows), 5).astype(BF16).reshape(OWNERS, 2, FIRST)

    copies[5].wait()
    copies[6].wait()
    groups = ELEMS // GROUP
    for t in range(groups + 1):
        if t < groups:
            for i in range(GROUP):
                blocks[GROUP * t + i].wait()
            for i in range(GROUP):
                diag_left(GROUP * t + i, dv, le, hs, t % 2, i)
        if t > 0:
            diag_right(GROUP * (t - 1), GROUP, hs, (t - 1) % 2, ri, gs)
        if t == 0:
            scatter(first, first_out, first_send, first_recv, 0)
        if GROUP * t == 6:
            half[...] = dot(pb[:, :6], diag_rows(gs, 0))
    placed = half[...] + dot(pb_late[:, :6], diag_rows(gs, 6))
    last[:, :, :SHARED] = placed[:, :SHARED].astype(BF16).reshape(OWNERS, 2, SHARED)
    step.wait()
    tail = packed(dot(pb[:, :16], minus[...]), 1, 64)
    tail = jnp.where(iota((16, MINUS), 1) < 64, jnp.concatenate([placed[:, SHARED:], tail[:, LANE:]], axis=1), tail)
    last[:, :, SHARED:] = tail.astype(BF16).reshape(OWNERS, 2, MINUS)
    scatter(last, last_out, last_send, last_recv, 1)
    planes = [pltpu.make_async_copy(ov.at[k], planes_out.at[k], plane_sem.at[k]) for k in range(5)]
    idx_copy.wait()

    @pl.when(jnp.logical_not(is_owner))
    def _():
        for k in range(5):
            ov[k] = jnp.zeros((SLOTS, 1600), BF16)
            planes[k].start()

    @pl.when(is_owner)
    def _():
        arrived(first, first_out, first_send, first_recv, 0)
        source = first_out[...].reshape(SLOTS, FIRST)
        for k in range(5):
            def store(at, value, k=k):
                ov[k, :, at] = value
            expand_block(plan, k + 1, source, idx_ref, store)
            planes[k].start()

    sent_all(first, first_out, first_send, first_recv)
    sent_all(last, last_out, last_send, last_recv)
    for p in planes:
        p.wait()

    @pl.when(is_owner)
    def _():
        arrived(last, last_out, last_send, last_recv, 1)


def expand(plan, planes_ref, last_ref, idx_ref, out_hbm, ov, sem):
    owner = lax.axis_index("grp") < OWNERS
    copies = [pltpu.make_async_copy(ov.at[k], out_hbm.at[k], sem.at[k]) for k in range(2)]
    copies += [pltpu.make_async_copy(planes_ref.at[k - 2], out_hbm.at[k], sem.at[k]) for k in range(2, 7)]
    for c in copies[2:]:
        c.start()

    @pl.when(jnp.logical_not(owner))
    def _():
        for k in range(2):
            ov[k] = jnp.zeros((SLOTS, 1600), BF16)
            copies[k].start()

    @pl.when(owner)
    def _():
        ov[0] = last_ref[:, :, :DIAG].reshape(SLOTS, DIAG)[:, :1600]
        copies[0].start()

        def store(at, value):
            ov[1, :, at] = value
        expand_block(plan, 0, last_ref[:, :, SHARED:].reshape(SLOTS, MINUS), idx_ref, store)
        copies[1].start()

    for c in copies:
        c.wait()


def shards(diag_jac, xface_jac, side_jac, orient, owner):
    tabs = tables()
    plan, idx = expand_tables()
    anys = pl.BlockSpec(memory_space=ANY)
    vm = pl.BlockSpec(memory_space=pltpu.VMEM)
    hbm = pl.BlockSpec(memory_space=pltpu.HBM)
    sds = jax.ShapeDtypeStruct
    dma = pltpu.SemaphoreType.DMA
    planes, last = pl.pallas_call(
        functools.partial(project_and_send, plan),
        out_shape=(sds((5, SLOTS, 1600), BF16), sds((GRP, 2, LAST), BF16)),
        in_specs=[hbm] * 11,
        out_specs=(anys, anys),
        scratch_shapes=[pltpu.SMEM((ELEMS,), jnp.int32), pltpu.SMEM((ELEMS,), jnp.int32),
                        pltpu.VMEM((ELEMS, 2, FLAT), BF16), pltpu.VMEM((ELEMS, 4, FLAT), BF16),
                        pltpu.VMEM((ELEMS, NF, NF), BF16)]
        + [pltpu.VMEM(t.shape, BF16) for t in tabs]
        + [pltpu.VMEM((ROWS, 16000), BF16), pltpu.VMEM((ROWS, ZT * LANE), F32),
           pltpu.VMEM((NV * 2 * ROWS, 512), BF16), pltpu.VMEM((2, 80 * GROUP, NF), BF16), pltpu.VMEM((480, LANE), F32),
           pltpu.VMEM((16, DIAG), F32), pltpu.VMEM((16, TILED), BF16), pltpu.VMEM((16, TILED), BF16),
           pltpu.VMEM((OWNERS, 2, FIRST), BF16), pltpu.VMEM((OWNERS, 2, LAST), BF16),
           pltpu.VMEM((GRP, 2, FIRST), BF16), pltpu.VMEM((5, SLOTS, 1600), BF16), pltpu.VMEM(idx.shape, jnp.int32),
           dma((22,)), dma((2,)), dma((5,)), dma, dma, dma((OWNERS,)), dma((GRP,)), dma((OWNERS,)), dma((GRP,))],
        compiler_params=pltpu.CompilerParams(collective_id=0, has_side_effects=True, vmem_limit_bytes=40 << 20),
        name="project_and_send",
    )(*[pltpu.with_memory_space_constraint(a, pltpu.HBM)
        for a in (orient, owner, xface_jac, side_jac, diag_jac, *tabs, idx)])
    planes = pl.pallas_call(
        functools.partial(expand, plan),
        out_shape=sds((7, SLOTS, 1600), BF16),
        in_specs=[vm, vm, vm],
        out_specs=hbm,
        scratch_shapes=[pltpu.VMEM((2, SLOTS, 1600), BF16), dma((7,))],
        compiler_params=pltpu.CompilerParams(vmem_limit_bytes=16 << 20),
        name="expand",
    )(planes, last, idx)
    return jnp.transpose(planes, (1, 0, 2))


def solution(mesh):
    split_all = P(("slab", "grp"), None, None)
    vector = P(("slab", "grp"))
    return jax.shard_map(shards, mesh=mesh, in_specs=(split_all, split_all, split_all, vector, vector),
                         out_specs=split_all, check_vma=False)
```
